512 devices in a mesh: guide: 2 (over core), dp: 16 (over y, x), mp: 16 (over z).
Axes of the slice: x: 4, y: 4, z: 16, core: 2. Of those that a mesh axis runs over, the one named last changes fastest.
Arguments:
- states: bfloat16 [2, 128, 2048], P('guide', 'dp'), may hold values from -6 to 6
- lengths: int32 [2, 128], P('guide', 'dp'), may hold values from 1 to 32768, as said below
- sink_cache: bfloat16 [2, 128, 16, 2, 4, 128], P('guide', 'dp', 'mp'), may hold values from -48 to 48
- window_cache: bfloat16 [2, 128, 16, 2, 256, 128], P('guide', 'dp', 'mp'), may hold values from -360 to 360
- qkv_weight: bfloat16 [2048, 3, 16, 128], P(None, None, 'mp'), may hold values from -0.125 to 0.125
- out_weight: bfloat16 [16, 128, 2048], P('mp'), may hold values from -0.125 to 0.125
- expert_ids: int32 [2, 128, 8], replicated, may hold values from 0 to 63, all different within a row; in each aligned block of 8 rows (0 to 7, 8 to 15, ..., all dimensions but the last counted through in order) at most 2 rows name the same one
- route_weight: float32 [2, 128, 8], replicated, may hold values from 0.5 to 2
- expert_in: bfloat16 [2, 2048, 65536], P(None, None, ('guide', 'dp', 'mp')), may hold values from -0.125 to 0.125
- expert_out: bfloat16 [65536, 2048], P(('guide', 'dp', 'mp')), may hold values from -0.1875 to 0.1875
- vocab_weight: bfloat16 [2048, 26624], P(('guide', 'dp'), 'mp'), may hold values from -0.125 to 0.125
- guidance: float32 [128], P('dp'), may hold values from 1 to 5
Outputs:
- guided: float32 [128, 16, 2, 832], P('dp', 'mp', 'guide')
The draws below stay inside these ranges and needn't reach their ends.
Inputs may be any that keep to these rules, and one draw needn't show every extreme that they name: `lengths`: one stream of one request has exactly 32768 cached positions. `expert_ids`: taking the tokens streams first, then requests, in aligned blocks of 8 tokens (the tokens of one device), no expert is named by more than 2 tokens of a block, a bound that some block reaches.
All inputs are finite; a program needn't handle non-finite values.
Results may differ from the reference program's by a relative error of at most 0.025.
Values may be sent and summed in bfloat16 or wider, within the bound.
A program may use at most 64 MiB of HBM per device.

```python
import math
import jax
import jax.numpy as jnp
import numpy as np
from jax import lax

D = 2048
HEADS = 16
HD = 128
EXPERTS = 64
FFE = 1024
TOPK = 8
MOST = 2
VOCAB = 26624
SINKS = 4
WINDOW = 256
MAXLEN = 32768
R_DEV = 8
REQUESTS = 128
N_MP = 16


def draw_lengths(key, part):
    key_exp, key_extra, key_pick = jax.random.split(key, 3)
    exponent = jax.random.randint(key_exp, (2, REQUESTS), 0, 15)
    base_len = jnp.left_shift(jnp.ones_like(exponent), exponent)
    extra_len = jax.random.randint(key_extra, (2, REQUESTS), 0, 16384) % base_len
    drawn_len = (base_len + extra_len).reshape(-1)
    pick_index = jax.random.randint(key_pick, (), 0, 2 * REQUESTS)
    return drawn_len.at[pick_index].set(MAXLEN).reshape(2, REQUESTS).astype(jnp.int32)


def draw_sink_cache(key, part):
    sample = jnp.clip(jax.random.normal(key, (2, REQUESTS, HEADS, 2, SINKS, HD), jnp.float32), -6.0, 6.0)
    factor = jnp.array([2.5, 8.0], jnp.float32).reshape(1, 1, 1, 2, 1, 1)
    return (sample * factor).astype(jnp.bfloat16)


def draw_window_cache(key, part):
    key_main = jax.random.fold_in(key, 0)
    sample = jnp.clip(jax.random.normal(key_main, (2, REQUESTS, HEADS, 2, WINDOW, HD), jnp.float32), -6.0, 6.0)
    factor = jnp.array([1.0, 8.0], jnp.float32).reshape(1, 1, 1, 2, 1, 1)
    return (sample * factor).astype(jnp.bfloat16)


def steps_of(own_key, dims, cuts, least, largest):
    loudness = 1.0
    for dim, shards_of in cuts:
        heights = jax.random.uniform(jax.random.fold_in(jax.random.fold_in(own_key, 6), dim), (shards_of,), jnp.float32, least / len(cuts), largest / len(cuts))
        loudness = loudness * jnp.repeat(jnp.exp(heights), dims[dim] // shards_of).reshape((-1,) + (1,) * (len(dims) - 1 - dim))
    return loudness


def shared_out(rng, own, number, rows, amount, top, limit, skew):
    sequence = jax.random.permutation(rng, amount)
    crowded, common = portions_of(amount, rows * top, limit, skew, True), portions_of(amount, rows * top, limit, skew, False)
    places = jnp.arange(amount)

    def named(tallies, turn):
        used = int((tallies > 0).sum())
        fixed = max(1, used // 4)
        shifted = fixed + (places - fixed + turn * (used - fixed)) % max(1, amount - fixed)
        return jnp.zeros((amount,), jnp.int32).at[sequence[jnp.where(places < fixed, places, shifted)]].set(jnp.asarray(tallies, jnp.int32))

    tallies = jnp.where(number % 4 == 0, named(crowded, number // 4), named(common, number - number // 4 - 1))
    mixed = jax.random.permutation(jax.random.fold_in(own, 3), amount)
    donor, sink = mixed[0:amount // 2 * 2:2], mixed[1:amount // 2 * 2:2]
    room = jnp.minimum(tallies[donor] - 1, limit - tallies[sink]) // 2
    room = jnp.where((donor == sequence[0]) | (sink == sequence[0]) | (tallies[sink] == 0), 0, jnp.maximum(room, 0))
    shifted = jax.random.randint(jax.random.fold_in(own, 4), (amount // 2,), 0, 1 << 20) % (room + 1)
    tallies = tallies.at[donor].add(-shifted).at[sink].add(shifted)
    members = jnp.searchsorted(jnp.cumsum(tallies), jnp.arange(rows * top), side="right").astype(jnp.int32)
    grid = members.reshape(top, rows).T
    grid = grid[jax.random.permutation(jax.random.fold_in(own, 1), rows)]
    turn = jax.random.randint(jax.random.fold_in(own, 2), (rows, 1), 0, top)
    return jnp.take_along_axis(grid, (jnp.arange(top)[None, :] + turn) % top, axis=1)


def portions_of(count, total, limit, slope, full):
    loads = [(1 << 20) // math.isqrt(rank ** slope) + 1 for rank in range(1, count + 1)]
    largest = limit if full else min(limit, max(-(-total // count), total * loads[0] // sum(loads)))
    least = 1 if total - largest >= count - 1 else 0
    counts, spare = [largest] + [least] * (count - 1), total - largest - least * (count - 1)
    while spare > 0:
        candidates = [i for i in range(1, count) if counts[i] < largest] or [i for i in range(1, count) if counts[i] < limit]
        pool, remaining = sum([loads[i] for i in candidates]), spare
        for i in candidates:
            addition = min(limit - counts[i], max(1, remaining * loads[i] // pool), spare)
            counts[i] = counts[i] + addition
            spare = spare - addition
    return np.array(counts)


def scatter_about(rng, dims, width, most, pieces=(), kind=jnp.bfloat16):
    values = width * jax.random.normal(rng, dims, jnp.float32)
    if pieces:
        values = values * steps_of(rng, dims, pieces, -0.22, 0.18)
    return jnp.clip(values, -most, most).astype(kind)


def setup_inputs(seed: int = 0) -> dict:
    keys = jax.random.split(jax.random.key(seed), 13)
    states = scatter_about(keys[0], (2, REQUESTS, D), 1.0, 6.0, ((0, 2), (1, 16)))
    lengths = draw_lengths(jax.random.fold_in(keys[12], 71), 0)
    sink_cache = draw_sink_cache(jax.random.fold_in(keys[12], 71), 0)
    window_cache = draw_window_cache(jax.random.fold_in(keys[12], 71), 0)
    qkv_weight = scatter_about(keys[4], (D, 3, HEADS, HD), D ** -0.5, 0.125, ((2, 16),))
    out_weight = scatter_about(keys[5], (HEADS, HD, D), (HEADS * HD) ** -0.5, 0.125, ((0, 16),))
    expert_ids_keys = jax.random.split(jax.random.fold_in(keys[6], 1), 2 * REQUESTS // R_DEV)
    expert_ids_turns = jax.random.permutation(jax.random.fold_in(keys[6], 3), 2 * REQUESTS // R_DEV)
    expert_ids = jax.vmap(lambda own, number: shared_out(jax.random.fold_in(keys[6], 2), own, number, R_DEV, EXPERTS, TOPK, MOST, 2))(expert_ids_keys, expert_ids_turns).reshape((2, REQUESTS, TOPK))
    route_weight = jnp.clip(jax.random.uniform(keys[7], (2, REQUESTS, TOPK), jnp.float32, 0.5, 2.0), 0.5, 2.0)
    expert_in = scatter_about(keys[8], (2, D, EXPERTS * FFE), D ** -0.5, 0.125, ((2, 512),))
    expert_out = scatter_about(keys[9], (EXPERTS * FFE, D), FFE ** -0.5, 0.1875, ((0, 512),))
    vocab_weight = scatter_about(keys[10], (D, VOCAB), D ** -0.5, 0.125, ((0, 32), (1, 16)))
    guidance = jnp.clip(1.0 + 4.0 * jax.random.uniform(keys[11], (REQUESTS,), jnp.float32) ** steps_of(keys[11], (REQUESTS,), ((0, 16),), -0.2, 0.2), 1.0, 5.0)
    return dict(states=states, lengths=lengths, sink_cache=sink_cache, window_cache=window_cache, qkv_weight=qkv_weight, out_weight=out_weight, expert_ids=expert_ids, route_weight=route_weight, expert_in=expert_in, expert_out=expert_out, vocab_weight=vocab_weight, guidance=guidance)


EPSILON = 1e-05

def rms_norm(values):
    return values * lax.rsqrt(lax.optimization_barrier(jnp.mean(values * values, axis=-1, keepdims=True)) + EPSILON)

def rotate(vectors, positions):
    full_width = vectors.shape[-1]
    half_width = full_width // 2
    step_index = jnp.arange(half_width, dtype=jnp.float32)
    inverse = jnp.exp(step_index * (-2.0 * math.log(10000.0) / full_width))
    angles = positions.astype(jnp.float32)[:, None] * inverse[None, :]
    cosine = jnp.cos(angles)[:, None, :]
    sine_part = jnp.sin(angles)[:, None, :]
    first_half = vectors[..., :half_width]
    second = vectors[..., half_width:]
    return jnp.concatenate([first_half * cosine - second * sine_part, second * cosine + first_half * sine_part], axis=-1)

def attend(operands, qkv_weight, out_weight):
    hidden, stream_lengths, sink_rows, window = operands
    normed = rms_norm(hidden.astype(jnp.float32)).astype(jnp.bfloat16)
    projected = jnp.einsum('rd,dthe->rthe', normed.astype(jnp.float32), qkv_weight.astype(jnp.float32))
    query_rot = rotate(projected[:, 0], stream_lengths).astype(jnp.bfloat16)
    fresh_key = rotate(projected[:, 1], stream_lengths).astype(jnp.bfloat16)
    fresh_value = projected[:, 2].astype(jnp.bfloat16)
    key_rows = jnp.concatenate([sink_rows[:, :, 0], window[:, :, 0], fresh_key[:, :, None]], axis=2)
    value_rows = jnp.concatenate([sink_rows[:, :, 1], window[:, :, 1], fresh_value[:, :, None]], axis=2)
    sink_count = sink_rows.shape[3]
    window_count = window.shape[3]
    scores = jnp.einsum('rhe,rhne->rhn', query_rot.astype(jnp.float32), key_rows.astype(jnp.float32)) / math.sqrt(query_rot.shape[-1])
    slot_index = jnp.arange(sink_count + window_count + 1, dtype=jnp.int32)[None, None, :]
    length_limit = stream_lengths.astype(jnp.int32)[:, None, None]
    valid_slot = jnp.where(slot_index < sink_count, slot_index < length_limit, jnp.where(slot_index < sink_count + window_count, slot_index >= 2 * sink_count + window_count - length_limit, True))
    scores = jnp.where(valid_slot, scores, -1e+30)
    weights = jax.nn.softmax(scores, axis=-1).astype(jnp.bfloat16)
    mixture = jnp.einsum('rhn,rhne->rhe', weights.astype(jnp.float32), value_rows.astype(jnp.float32)).astype(jnp.bfloat16)
    output = jnp.einsum('rhe,hed->rd', mixture.astype(jnp.float32), out_weight.astype(jnp.float32))
    return (hidden.astype(jnp.float32) + output).astype(jnp.bfloat16)

def reference(states, lengths, sink_cache, window_cache, qkv_weight, out_weight, expert_ids, route_weight, expert_in, expert_out, vocab_weight, guidance):
    after_attention = lax.map(lambda operands: attend(operands, qkv_weight, out_weight), (states, lengths, sink_cache, window_cache))
    tokens_total = states.shape[0] * states.shape[1]
    model_width = states.shape[2]
    residual = after_attention.reshape(tokens_total, model_width)
    moe_in = rms_norm(residual.astype(jnp.float32)).astype(jnp.bfloat16)
    choice_rows = expert_ids.reshape(tokens_total, -1)
    route_rows = route_weight.reshape(tokens_total, -1)
    inputs_by_expert = expert_in.reshape(2, model_width, EXPERTS, FFE).transpose(2, 0, 1, 3)
    outputs_by_expert = expert_out.reshape(EXPERTS, FFE, model_width)

    def expert_step(running, operands):
        expert_index, weights_in, weights_out = operands
        coefficient = lax.optimization_barrier(jnp.sum(jnp.where(choice_rows == expert_index, route_rows, 0.0), axis=-1))
        gate = jnp.dot(moe_in, weights_in[0], preferred_element_type=jnp.float32)
        upward = jnp.dot(moe_in, weights_in[1], preferred_element_type=jnp.float32)
        activated = (jax.nn.silu(gate) * upward * coefficient[:, None]).astype(jnp.bfloat16)
        return (running + jnp.dot(activated, weights_out, preferred_element_type=jnp.float32), None)
    initial = jnp.zeros((tokens_total, model_width), jnp.float32)
    expert_sum, unused = lax.scan(expert_step, initial, (jnp.arange(EXPERTS, dtype=jnp.int32), inputs_by_expert, outputs_by_expert))
    final = rms_norm(residual.astype(jnp.float32) + expert_sum).astype(jnp.bfloat16)
    logits = jnp.dot(final, vocab_weight, preferred_element_type=jnp.float32).reshape(2, states.shape[1], -1)
    guided = logits[1] + guidance[:, None] * (logits[0] - logits[1])
    return guided.reshape(states.shape[1], N_MP, 2, VOCAB // (2 * N_MP))
```

```python
import math

import jax
import jax.numpy as jnp
from jax import lax
from jax.experimental import pallas as pl
from jax.experimental.pallas import tpu as pltpu
from jax.sharding import PartitionSpec as P

F32 = jnp.float32
BF16 = jnp.bfloat16
EPSILON = 1e-05
MESH = pl.DeviceIdType.MESH
D = 2048
HD = 128
R = 8
NZ = 16
ND = 16
NP = 32
SINKS = 4
WINDOW = 256
HALF = 832
WIDE = 896
NEG = -1e30


def iota(shape, axis):
    return lax.broadcasted_iota(jnp.int32, shape, axis)


def dot(a, b):
    return jnp.dot(a, b, preferred_element_type=F32)


def dot_nt(a, b):
    return lax.dot_general(a, b, (((1,), (1,)), ((), ())), preferred_element_type=F32)


def column(row):
    square = jnp.broadcast_to(row, (R, R))
    return jnp.sum(jnp.where(iota((R, R), 0) == iota((R, R), 1), square, 0.0), axis=1, keepdims=True)


def kernel(
    states_h, lengths_h, sink_h, window_h, qkv_h, outw_h, ids_h, route_h, ein_h, eout_h, vocab_h, guid_h,
    out_ref,
    st_v, len_v, sink_v, sinkf_v, k_v, v_v, qkv_v, outw_v, ids_v, rw_v, ein_v, eout_v, voc_v, gd_v,
    send1, recv1, rz, send3, recv3, send4, recv4, send5, recv5, uz, send7, recv7, send8, recv8,
    local_sem, send_sem, recv_sem,
):
    g = lax.axis_index("guide")
    d = lax.axis_index("dp")
    m = lax.axis_index("mp")
    me = g * ND + d

    loads = {}

    def load(name, src, dst):
        copy = pltpu.make_async_copy(src, dst, local_sem.at[len(loads)])
        loads[name] = copy
        copy.start()

    load("states", states_h.at[0], st_v)
    load("lengths", lengths_h, len_v)
    for t in range(3):
        load("qkv%d" % t, qkv_h.at[t], qkv_v.at[:, pl.ds(t * HD, HD)])
    load("sink", sink_h.at[0, :, 0], sink_v)
    load("k", window_h.at[0, :, 0, 0], k_v)
    load("v", window_h.at[0, :, 0, 1], v_v)
    load("outw", outw_h.at[0], outw_v)
    load("ids", ids_h, ids_v)
    load("route", route_h, rw_v)
    load("ein0", ein_h.at[0], ein_v.at[:, pl.ds(0, HD)])
    load("ein1", ein_h.at[1], ein_v.at[:, pl.ds(HD, HD)])
    load("eout", eout_h, eout_v)
    half_start = pl.multiple_of(lax.rem(d, 2) * 64, 64)
    other_start = pl.multiple_of((1 - lax.rem(d, 2)) * 64, 64)
    load("voc0", vocab_h.at[:, pl.ds(0, WIDE)], voc_v.at[0, pl.ds(half_start, 64), :])
    load("voc1", vocab_h.at[:, pl.ds(768, WIDE)], voc_v.at[1, pl.ds(half_start, 64), :])
    load("guid", guid_h, gd_v)

    barrier = pltpu.get_barrier_semaphore()

    def plane_peer(i):
        k = lax.rem(me + i, NP)
        return k, (k // ND, lax.rem(k, ND), m)

    def z_peer(i):
        k = lax.rem(m + i, NZ)
        return k, (g, d, k)

    def greet_z(i, carry):
        pl.semaphore_signal(barrier, inc=1, device_id=z_peer(i)[1], device_id_type=MESH)
        return carry

    def greet_plane(i, carry):
        pl.semaphore_signal(barrier, inc=1, device_id=plane_peer(i)[1], device_id_type=MESH)
        return carry

    lax.fori_loop(1, NZ, greet_z, 0)
    lax.fori_loop(1, NP, greet_plane, 0)

    def remote(phase, src, dst, device):
        pltpu.make_async_remote_copy(
            src_ref=src, dst_ref=dst, send_sem=send_sem.at[phase], recv_sem=recv_sem.at[phase],
            device_id=device, device_id_type=MESH,
        ).start()

    def arrived(phase, ref):
        pltpu.make_async_copy(ref, ref, recv_sem.at[phase]).wait()

    def sent(phase, ref):
        pltpu.make_async_copy(ref, ref, send_sem.at[phase]).wait()

    step_index = lax.rem(iota((1, HD), 1), HD // 2).astype(F32)
    inverse = jnp.exp(step_index * (-2.0 * math.log(10000.0) / HD))
    loads["lengths"].wait()
    position = column(len_v[...].astype(F32))
    angles = position * inverse
    cosine = jnp.cos(angles)
    sine = jnp.sin(angles)
    sine = jnp.where(iota((R, HD), 1) < HD // 2, -sine, sine)
    loads["states"].wait()
    hidden = st_v[...].astype(F32)
    normed = (hidden * lax.rsqrt(jnp.mean(hidden * hidden, axis=-1, keepdims=True) + EPSILON)).astype(BF16)
    loads["sink"].wait()
    for r in range(R):
        for t in range(2):
            sinkf_v[pl.ds(t * R * SINKS + r * SINKS, SINKS), :] = sink_v[r, t].astype(F32)
    for t in range(3):
        loads["qkv%d" % t].wait()
    projected = dot(normed, qkv_v[...])
    query = projected[:, :HD]
    key = projected[:, HD : 2 * HD]
    query = (query * cosine + pltpu.roll(query, HD // 2, axis=1) * sine).astype(BF16)
    key = (key * cosine + pltpu.roll(key, HD // 2, axis=1) * sine).astype(BF16)
    fresh = projected[:, 2 * HD :].astype(BF16)
    root = 1.0 / math.sqrt(HD)
    sinks = sinkf_v[...].astype(BF16)
    loads["k"].wait()
    window_scores = dot_nt(query, k_v[...].reshape(R * WINDOW, HD)) * root
    sink_scores = dot_nt(query, sinks[: R * SINKS]) * root
    self_scores = jnp.sum(query.astype(F32) * key.astype(F32), axis=1, keepdims=True) * root
    position_i = position.astype(jnp.int32)
    slot = iota((R, R * WINDOW), 1)
    window_ok = (slot // WINDOW == iota((R, R * WINDOW), 0)) & (
        lax.rem(slot, WINDOW) >= SINKS + WINDOW - position_i
    )
    slot = iota((R, R * SINKS), 1)
    sink_ok = (slot // SINKS == iota((R, R * SINKS), 0)) & (lax.rem(slot, SINKS) < position_i)
    window_scores = jnp.where(window_ok, window_scores, NEG)
    sink_scores = jnp.where(sink_ok, sink_scores, NEG)
    highest = jnp.maximum(
        jnp.maximum(
            jnp.max(window_scores, axis=1, keepdims=True), jnp.max(sink_scores, axis=1, keepdims=True)
        ),
        self_scores,
    )
    window_exp = jnp.where(window_ok, jnp.exp(window_scores - highest), 0.0)
    sink_exp = jnp.where(sink_ok, jnp.exp(sink_scores - highest), 0.0)
    self_exp = jnp.exp(self_scores - highest)
    total = jnp.sum(window_exp, axis=1, keepdims=True) + jnp.sum(sink_exp, axis=1, keepdims=True) + self_exp
    scale = 1.0 / total
    window_prob = (window_exp * scale).astype(BF16)
    sink_prob = (sink_exp * scale).astype(BF16)
    self_prob = (self_exp * scale).astype(BF16).astype(F32)
    loads["v"].wait()
    mixture = (
        dot(window_prob, v_v[...].reshape(R * WINDOW, HD))
        + dot(sink_prob, sinks[R * SINKS :])
        + self_prob * fresh.astype(F32)
    ).astype(BF16)
    loads["outw"].wait()
    partial = dot(mixture, outw_v[...])
    for j in range(NZ):
        send1[j] = partial[:, j * HD : (j + 1) * HD].astype(BF16)

    pl.semaphore_wait(barrier, NZ - 1 + NP - 1)

    def send_1(i, carry):
        k, device = z_peer(i)
        remote(0, send1.at[k], recv1.at[i - 1], device)
        return carry

    lax.fori_loop(1, NZ, send_1, 0)

    loads["ids"].wait()
    loads["route"].wait()
    half = m // (NZ // 2)
    own_expert = 2 * me + half
    before = (iota((HD, HD), 0) // R == iota((HD, HD), 1) // R) & (iota((HD, HD), 0) < iota((HD, HD), 1))
    before = jnp.where(before, 1.0, 0.0).astype(BF16)
    coefficients = []
    for s in range(2):
        match = ids_v[s] == own_expert
        chosen = jnp.sum(jnp.where(match, 1.0, 0.0), axis=0, keepdims=True)
        weight = jnp.sum(jnp.where(match, rw_v[s], 0.0), axis=0, keepdims=True)
        rank = dot(jnp.broadcast_to(chosen, (R, HD)).astype(BF16), before)[:1]
        rows, lanes = iota((32, HD), 0), iota((32, HD), 1)
        takes = (lanes // R == rows // 2) & (rank.astype(jnp.int32) == lax.rem(rows, 2)) & (chosen > 0.5)
        coefficients.append(jnp.sum(jnp.where(takes, weight, 0.0), axis=1, keepdims=True))
    coefficient = jnp.concatenate(coefficients, axis=0)

    own_ids = jnp.where(g == 0, ids_v[0], ids_v[1]).astype(F32).astype(BF16)
    pick = jnp.where(iota((HD, 64), 0) == d * R + lax.rem(iota((HD, 64), 1), R), 1.0, 0.0).astype(BF16)
    ids_row = dot(own_ids, pick)
    pick = jnp.where(iota((64, HD), 1) == d * R + lax.rem(iota((64, HD), 0), R), 1.0, 0.0).astype(BF16)
    ids_col = dot_nt(pick, own_ids)
    rows = iota((512, 64), 0)
    cols = iota((512, 64), 1)
    expert = (rows // 16 * 2 + half).astype(F32)
    named = jnp.zeros((512, 64), F32)
    for i in range(8):
        named = jnp.where(expert == ids_row[i : i + 1, :], 1.0, named)
    earlier = (iota((64, 64), 0) // R == iota((64, 64), 1) // R) & (iota((64, 64), 0) < iota((64, 64), 1))
    rank = dot(named.astype(BF16), jnp.where(earlier, 1.0, 0.0).astype(BF16))
    scatter = jnp.where(
        (named > 0.5) & (rank.astype(jnp.int32) == lax.rem(rows // 8, 2)) & (lax.rem(rows, 8) == cols // R), 1.0, 0.0
    ).astype(BF16)
    rows = iota((64, 512), 0)
    cols = iota((64, 512), 1)
    expert = (cols // 16 * 2 + half).astype(F32)
    named = jnp.zeros((64, 512), F32)
    for i in range(8):
        named = jnp.where(expert == ids_col[:, i : i + 1], 1.0, named)
    earlier = (iota((64, 64), 0) // R == iota((64, 64), 1) // R) & (iota((64, 64), 1) < iota((64, 64), 0))
    rank = dot(jnp.where(earlier, 1.0, 0.0).astype(BF16), named.astype(BF16))
    gather = jnp.where(
        (named > 0.5) & (rank.astype(jnp.int32) == lax.rem(cols // 8, 2)) & (lax.rem(cols, 8) == rows // R), 1.0, 0.0
    ).astype(BF16)
    rows, cols = iota((64, 64), 0), iota((64, 64), 1)
    swap = jnp.where((rows // 8 == lax.rem(cols, 8)) & (lax.rem(rows, 8) == cols // 8), 1.0, 0.0).astype(BF16)
    voc_v[:, pl.ds(other_start, 64), :] = jnp.zeros((2, 64, WIDE), BF16)

    own_partial = send1[m].astype(F32)
    own_states = st_v[:, pl.ds(pl.multiple_of(m * HD, HD), HD)].astype(F32)
    arrived(0, recv1)
    summed = own_partial + jnp.sum(recv1[...].astype(F32), axis=0)
    residual_chunk = (own_states + summed).astype(BF16)
    rz[m] = residual_chunk

    def send_2(i, carry):
        k, device = z_peer(i)
        remote(1, rz.at[m], rz.at[m], device)
        return carry

    lax.fori_loop(1, NZ, send_2, 0)
    arrived(1, rz.at[pl.ds(0, NZ - 1)])
    pieces = [
        jnp.concatenate([rz[2 * q].astype(F32), rz[2 * q + 1].astype(F32)], axis=1) for q in range(8)
    ]
    squares = sum(jnp.sum(p * p, axis=1, keepdims=True) for p in pieces)
    inv = lax.rsqrt(squares / D + EPSILON)
    stacked = jnp.concatenate([p * inv for p in pieces], axis=0).astype(BF16)

    send3[...] = dot(scatter, stacked).astype(BF16).reshape(NP, 16, 256)

    def send_3(i, carry):
        k, device = plane_peer(i)
        remote(2, send3.at[k], recv3.at[me], device)
        return carry

    lax.fori_loop(1, NP, send_3, 0)
    recv3[me] = send3[me]
    for name in ("ein0", "ein1", "eout"):
        loads[name].wait()
    arrived(2, recv3.at[pl.ds(0, NP - 1)])
    tokens = []
    for n in range(8):
        turned = dot(swap, recv3[4 * n : 4 * n + 4].reshape(64, 256))
        tokens.append(jnp.concatenate([turned[8 * q : 8 * q + 8] for q in range(8)], axis=1))
    tokens = jnp.concatenate(tokens, axis=0).astype(BF16)
    both = dot(tokens, ein_v[...])
    gate, upward = both[:, :HD], both[:, HD:]
    activated = (gate / (1.0 + jnp.exp(-gate)) * upward * coefficient).astype(BF16)
    terms = dot(activated, eout_v[...])
    for n in range(8):
        part = terms[8 * n : 8 * n + 8]
        part = jnp.concatenate([part[:, 256 * q : 256 * q + 256] for q in range(8)], axis=0).astype(BF16)
        send4[4 * n : 4 * n + 4] = dot(swap, part).astype(BF16).reshape(4, 16, 256)

    def send_4(i, carry):
        k, device = plane_peer(i)
        remote(3, send4.at[k], recv4.at[me], device)
        return carry

    lax.fori_loop(1, NP, send_4, 0)
    recv4[me] = send4[me]
    arrived(3, recv4.at[pl.ds(0, NP - 1)])
    own_terms = dot(gather, recv4[...].reshape(512, 256))
    for j in range(NZ):
        send5[j] = own_terms[j // 2 * 8 : j // 2 * 8 + 8, j % 2 * HD : j % 2 * HD + HD].astype(BF16)

    def send_5(i, carry):
        k, device = z_peer(i)
        remote(4, send5.at[k], recv5.at[i - 1], device)
        return carry

    lax.fori_loop(1, NZ, send_5, 0)
    own_sum = residual_chunk.astype(F32) + send5[m].astype(F32)
    arrived(4, recv5)
    uz[m] = (own_sum + jnp.sum(recv5[...].astype(F32), axis=0)).astype(BF16)

    def send_6(i, carry):
        k, device = z_peer(i)
        remote(5, uz.at[m], uz.at[m], device)
        return carry

    lax.fori_loop(1, NZ, send_6, 0)
    loads["guid"].wait()
    guidance = column(gd_v[...])
    share = jnp.where(g == 0, guidance, 1.0 - guidance)
    arrived(5, uz.at[pl.ds(0, NZ - 1)])
    pieces = [uz[j].astype(F32) for j in range(NZ)]
    squares = sum(jnp.sum(p * p, axis=1, keepdims=True) for p in pieces)
    inv = lax.rsqrt(squares / D + EPSILON)
    for j in range(NZ):
        send7[j] = (pieces[j] * inv).astype(BF16).astype(F32) * share

    def send_7(i, carry):
        k, device = plane_peer(i)
        remote(6, send7.at[k // 2], recv7.at[me], device)
        return carry

    lax.fori_loop(1, NP, send_7, 0)
    recv7[me] = send7[me // 2]
    loads["voc0"].wait()
    loads["voc1"].wait()
    arrived(6, recv7.at[pl.ds(0, NP - 1)])
    mixed = (recv7[:ND] + recv7[ND:]).reshape(ND * R, HD).astype(BF16)
    for c in range(2):
        send8[c * ND : (c + 1) * ND] = dot(mixed, voc_v[c]).reshape(ND, R, WIDE).astype(BF16)

    def send_8(i, carry):
        k, device = plane_peer(i)
        remote(7, send8.at[k], recv8.at[me], device)
        return carry

    lax.fori_loop(1, NP, send_8, 0)
    recv8[me] = send8[me]
    arrived(7, recv8.at[pl.ds(0, NP - 1)])
    logits = jnp.sum(recv8[...].astype(F32), axis=0)
    logits = jnp.where(g == 0, logits, pltpu.roll(logits, WIDE - 64, axis=1))
    out_ref[...] = logits[:, :HALF]

    sent(0, recv1)
    sent(1, recv1)
    sent(2, recv3.at[pl.ds(0, NP - 1)])
    sent(3, recv4.at[pl.ds(0, NP - 1)])
    sent(4, recv5)
    sent(5, recv5)
    sent(6, recv7.at[pl.ds(0, NP - 1)])
    sent(7, recv8.at[pl.ds(0, NP - 1)])


def body(
    states, lengths, sink_cache, window_cache, qkv_weight, out_weight, expert_ids, route_weight,
    expert_in, expert_out, vocab_weight, guidance,
):
    qkv = jnp.transpose(qkv_weight, (1, 2, 0, 3)).reshape(3, D, HD)
    ids = jnp.transpose(expert_ids, (0, 2, 1))
    route = jnp.transpose(route_weight, (0, 2, 1))
    guided = pl.pallas_call(
        kernel,
        out_shape=jax.ShapeDtypeStruct((R, HALF), F32),
        in_specs=[pl.BlockSpec(memory_space=pl.ANY)] * 12,
        out_specs=pl.BlockSpec(memory_space=pltpu.VMEM),
        scratch_shapes=[
            pltpu.VMEM((R, D), BF16),
            pltpu.VMEM((1, R), jnp.int32),
            pltpu.VMEM((R, 2, SINKS, HD), BF16),
            pltpu.VMEM((2 * R * SINKS, HD), F32),
            pltpu.VMEM((R, WINDOW, HD), BF16),
            pltpu.VMEM((R, WINDOW, HD), BF16),
            pltpu.VMEM((D, 3 * HD), BF16),
            pltpu.VMEM((HD, D), BF16),
            pltpu.VMEM((2, 8, HD), jnp.int32),
            pltpu.VMEM((2, 8, HD), F32),
            pltpu.VMEM((D, 2 * HD), BF16),
            pltpu.VMEM((HD, D), BF16),
            pltpu.VMEM((2, HD, WIDE), BF16),
            pltpu.VMEM((1, R), F32),
            pltpu.VMEM((NZ, R, HD), BF16),
            pltpu.VMEM((NZ - 1, R, HD), BF16),
            pltpu.VMEM((NZ, R, HD), BF16),
            pltpu.VMEM((NP, 16, 256), BF16),
            pltpu.VMEM((NP, 16, 256), BF16),
            pltpu.VMEM((NP, 16, 256), BF16),
            pltpu.VMEM((NP, 16, 256), BF16),
            pltpu.VMEM((NZ, R, HD), BF16),
            pltpu.VMEM((NZ - 1, R, HD), BF16),
            pltpu.VMEM((NZ, R, HD), BF16),
            pltpu.VMEM((NZ, R, HD), F32),
            pltpu.VMEM((NP, R, HD), F32),
            pltpu.VMEM((NP, R, WIDE), BF16),
            pltpu.VMEM((NP, R, WIDE), BF16),
            pltpu.SemaphoreType.DMA((17,)),
            pltpu.SemaphoreType.DMA((8,)),
            pltpu.SemaphoreType.DMA((8,)),
        ],
        compiler_params=pltpu.CompilerParams(
            collective_id=0, has_side_effects=True, vmem_limit_bytes=56 << 20
        ),
    )(
        states, lengths, sink_cache, window_cache, qkv, out_weight, ids, route,
        expert_in, expert_out, vocab_weight, guidance.reshape(1, R),
    )
    return guided.reshape(R, 1, 1, HALF)


def solution(mesh):
    in_specs = (
        P("guide", "dp", None),
        P("guide", "dp"),
        P("guide", "dp", "mp", None, None, None),
        P("guide", "dp", "mp", None, None, None),
        P(None, None, "mp", None),
        P("mp", None, None),
        P(),
        P(),
        P(None, None, ("guide", "dp", "mp")),
        P(("guide", "dp", "mp"), None),
        P(("guide", "dp"), "mp"),
        P("dp"),
    )
    out_specs = P("dp", "mp", "guide", None)
    return jax.shard_map(body, mesh=mesh, in_specs=in_specs, out_specs=out_specs, check_vma=False)
```

```python
import math

import jax
import jax.numpy as jnp
from jax import lax
from jax.experimental import pallas as pl
from jax.experimental.pallas import tpu as pltpu
from jax.sharding import PartitionSpec as P

F32 = jnp.float32
BF16 = jnp.bfloat16
EPSILON = 1e-05
MESH = pl.DeviceIdType.MESH
D = 2048
HD = 128
R = 8
NZ = 16
ND = 16
NP = 32
NC = 8
SINKS = 4
WINDOW = 256
HALF = 832
WIDE = 896
NEG = -1e30


def iota(shape, axis):
    return lax.broadcasted_iota(jnp.int32, shape, axis)


def dot(a, b):
    return jnp.dot(a, b, preferred_element_type=F32)


def dot_nt(a, b):
    return lax.dot_general(a, b, (((1,), (1,)), ((), ())), preferred_element_type=F32)


def column(row):
    square = jnp.broadcast_to(row, (R, R))
    return jnp.sum(jnp.where(iota((R, R), 0) == iota((R, R), 1), square, 0.0), axis=1, keepdims=True)


def kernel(
    states_h, lengths_h, sink_h, window_h, qkv_h, outw_h, ids_h, route_h, ein_h, eout_h, vocab_h, guid_h,
    out_ref,
    st_v, len_v, sink_v, sinkf_v, k_v, v_v, qkv_v, outw_v, ids_v, rw_v, ein_v, eout_v, voc_v, gd_v,
    send1, recv1, rz, send3, recv3, send4, recv4, send5, recv5, uz, send7, recv7, send8, recv8,
    local_sem, send_sem, recv_sem,
):
    g = lax.axis_index("guide")
    d = lax.axis_index("dp")
    m = lax.axis_index("mp")
    me = g * ND + d

    barrier = pltpu.get_barrier_semaphore()

    y, x = d // 4, lax.rem(d, 4)

    def turn(a):
        return jnp.where(a == 0, 2, jnp.where(a == 1, 1, jnp.where(a == 2, 3, 0)))

    def chip(i):
        return lax.rem(y + turn(i // 4), 4) * 4 + lax.rem(x + turn(lax.rem(i, 4)), 4)

    def to_chips(act):
        def step(i, carry):
            other = chip(i)
            act(g, other)
            return carry

        lax.fori_loop(0, ND - 1, step, 0)

    def to_plane(act):
        def step(i, carry):
            other = chip(i)
            act(0, other)
            act(1, other)
            return carry

        lax.fori_loop(0, ND - 1, step, 0)
        act(1 - g, d)

    def to_mp(act):
        def step(i, carry):
            offset = jnp.where(lax.rem(i, 2) == 0, 8 + i // 2, 8 - (i + 1) // 2)
            act(lax.rem(m + offset, NZ))
            return carry

        lax.fori_loop(0, NZ - 1, step, 0)

    def to_near_mp(act):
        def step(i, carry):
            offset = jnp.where(lax.rem(i, 2) == 0, 4 - i // 2, 13 + i // 2)
            act(lax.rem(m + offset, NZ))
            return carry

        lax.fori_loop(0, NC - 1, step, 0)

    def greet(device):
        pl.semaphore_signal(barrier, inc=1, device_id=device, device_id_type=MESH)

    to_mp(lambda k: greet((g, d, k)))
    to_plane(lambda p, q: greet((p, q, m)))

    loads = {}

    def load(name, src, dst):
        copy = pltpu.make_async_copy(src, dst, local_sem.at[len(loads)])
        loads[name] = copy
        copy.start()

    load("states", states_h.at[0], st_v)
    load("lengths", lengths_h, len_v)
    for t in range(3):
        load("qkv%d" % t, qkv_h.at[t], qkv_v.at[:, pl.ds(t * HD, HD)])
    load("sink", sink_h.at[0, :, 0], sink_v)
    load("k", window_h.at[0, :, 0, 0], k_v)
    load("v", window_h.at[0, :, 0, 1], v_v)
    load("outw", outw_h.at[0], outw_v)
    load("ids", ids_h, ids_v)
    load("route", route_h, rw_v)
    load("ein0", ein_h.at[0], ein_v.at[:, pl.ds(0, HD)])
    load("ein1", ein_h.at[1], ein_v.at[:, pl.ds(HD, HD)])
    load("eout", eout_h, eout_v)
    own_columns = pl.ds(pl.multiple_of(g * 768, HD), WIDE)
    own_rows = pl.ds(pl.multiple_of(g * 64, 64), 64)
    load("vocab", vocab_h.at[:, own_columns], voc_v.at[own_rows, :])
    load("guid", guid_h, gd_v)

    def remote(phase, src, dst, device):
        pltpu.make_async_remote_copy(
            src_ref=src, dst_ref=dst, send_sem=send_sem.at[phase], recv_sem=recv_sem.at[phase],
            device_id=device, device_id_type=MESH,
        ).start()

    def arrived(phase, ref):
        pltpu.make_async_copy(ref, ref, recv_sem.at[phase]).wait()

    def sent(phase, ref):
        pltpu.make_async_copy(ref, ref, send_sem.at[phase]).wait()

    step_index = lax.rem(iota((1, HD), 1), HD // 2).astype(F32)
    inverse = jnp.exp(step_index * (-2.0 * math.log(10000.0) / HD))
    loads["lengths"].wait()
    position = column(len_v[...].astype(F32))
    angles = position * inverse
    cosine = jnp.cos(angles)
    sine = jnp.sin(angles)
    sine = jnp.where(iota((R, HD), 1) < HD // 2, -sine, sine)
    loads["states"].wait()
    hidden = st_v[...].astype(F32)
    normed = (hidden * lax.rsqrt(jnp.mean(hidden * hidden, axis=-1, keepdims=True) + EPSILON)).astype(BF16)
    loads["sink"].wait()
    for r in range(R):
        for t in range(2):
            sinkf_v[pl.ds(t * R * SINKS + r * SINKS, SINKS), :] = sink_v[r, t].astype(F32)
    for t in range(3):
        loads["qkv%d" % t].wait()
    projected = dot(normed, qkv_v[...])
    query = projected[:, :HD]
    key = projected[:, HD : 2 * HD]
    query = (query * cosine + pltpu.roll(query, HD // 2, axis=1) * sine).astype(BF16)
    key = (key * cosine + pltpu.roll(key, HD // 2, axis=1) * sine).astype(BF16)
    fresh = projected[:, 2 * HD :].astype(BF16)
    root = 1.0 / math.sqrt(HD)
    sinks = sinkf_v[...].astype(BF16)
    loads["k"].wait()
    window_scores = dot_nt(query, k_v[...].reshape(R * WINDOW, HD)) * root
    sink_scores = dot_nt(query, sinks[: R * SINKS]) * root
    self_scores = jnp.sum(query.astype(F32) * key.astype(F32), axis=1, keepdims=True) * root
    position_i = position.astype(jnp.int32)
    slot = iota((R, R * WINDOW), 1)
    window_ok = (slot // WINDOW == iota((R, R * WINDOW), 0)) & (
        lax.rem(slot, WINDOW) >= SINKS + WINDOW - position_i
    )
    slot = iota((R, R * SINKS), 1)
    sink_ok = (slot // SINKS == iota((R, R * SINKS), 0)) & (lax.rem(slot, SINKS) < position_i)
    window_scores = jnp.where(window_ok, window_scores, NEG)
    sink_scores = jnp.where(sink_ok, sink_scores, NEG)
    highest = jnp.maximum(
        jnp.maximum(
            jnp.max(window_scores, axis=1, keepdims=True), jnp.max(sink_scores, axis=1, keepdims=True)
        ),
        self_scores,
    )
    window_exp = jnp.where(window_ok, jnp.exp(window_scores - highest), 0.0)
    sink_exp = jnp.where(sink_ok, jnp.exp(sink_scores - highest), 0.0)
    self_exp = jnp.exp(self_scores - highest)
    total = jnp.sum(window_exp, axis=1, keepdims=True) + jnp.sum(sink_exp, axis=1, keepdims=True) + self_exp
    scale = 1.0 / total
    window_prob = (window_exp * scale).astype(BF16)
    sink_prob = (sink_exp * scale).astype(BF16)
    self_prob = (self_exp * scale).astype(BF16).astype(F32)
    loads["v"].wait()
    mixture = (
        dot(window_prob, v_v[...].reshape(R * WINDOW, HD))
        + dot(sink_prob, sinks[R * SINKS :])
        + self_prob * fresh.astype(F32)
    ).astype(BF16)
    loads["outw"].wait()
    partial = dot(mixture, outw_v[...])
    for j in range(NC):
        send1[j] = partial[:, j * 256 : (j + 1) * 256].astype(BF16)
    chunk = lax.rem(m, NC)

    pl.semaphore_wait(barrier, NZ - 1 + NP - 1)

    to_mp(lambda k: remote(0, send1.at[lax.rem(k, NC)], recv1.at[m], (g, d, k)))
    recv1[m] = send1[chunk]
    remote(8, vocab_h.at[:, pl.ds(pl.multiple_of((1 - g) * 768, HD), WIDE)], voc_v.at[own_rows, :], (1 - g, d, m))

    loads["ids"].wait()
    loads["route"].wait()
    half = m // (NZ // 2)
    own_expert = 2 * me + half
    before = (iota((HD, HD), 0) // R == iota((HD, HD), 1) // R) & (iota((HD, HD), 0) < iota((HD, HD), 1))
    before = jnp.where(before, 1.0, 0.0).astype(BF16)
    coefficients = []
    for s in range(2):
        match = ids_v[s] == own_expert
        chosen = jnp.sum(jnp.where(match, 1.0, 0.0), axis=0, keepdims=True)
        weight = jnp.sum(jnp.where(match, rw_v[s], 0.0), axis=0, keepdims=True)
        rank = dot(jnp.broadcast_to(chosen, (R, HD)).astype(BF16), before)[:1]
        rows, lanes = iota((32, HD), 0), iota((32, HD), 1)
        takes = (lanes // R == rows // 2) & (rank.astype(jnp.int32) == lax.rem(rows, 2)) & (chosen > 0.5)
        coefficients.append(jnp.sum(jnp.where(takes, weight, 0.0), axis=1, keepdims=True))
    coefficient = jnp.concatenate(coefficients, axis=0)

    own_ids = jnp.where(g == 0, ids_v[0], ids_v[1]).astype(F32).astype(BF16)
    pick = jnp.where(iota((HD, 64), 0) == d * R + lax.rem(iota((HD, 64), 1), R), 1.0, 0.0).astype(BF16)
    ids_row = dot(own_ids, pick)
    pick = jnp.where(iota((64, HD), 1) == d * R + lax.rem(iota((64, HD), 0), R), 1.0, 0.0).astype(BF16)
    ids_col = dot_nt(pick, own_ids)
    rows = iota((512, 64), 0)
    cols = iota((512, 64), 1)
    expert = (rows // 16 * 2 + half).astype(F32)
    named = jnp.zeros((512, 64), F32)
    for i in range(8):
        named = jnp.where(expert == ids_row[i : i + 1, :], 1.0, named)
    earlier = (iota((64, 64), 0) // R == iota((64, 64), 1) // R) & (iota((64, 64), 0) < iota((64, 64), 1))
    rank = dot(named.astype(BF16), jnp.where(earlier, 1.0, 0.0).astype(BF16))
    scatter = jnp.where(
        (named > 0.5) & (rank.astype(jnp.int32) == lax.rem(rows // 8, 2)) & (lax.rem(rows, 8) == cols // R), 1.0, 0.0
    ).astype(BF16)
    rows = iota((64, 512), 0)
    cols = iota((64, 512), 1)
    expert = (cols // 16 * 2 + half).astype(F32)
    named = jnp.zeros((64, 512), F32)
    for i in range(8):
        named = jnp.where(expert == ids_col[:, i : i + 1], 1.0, named)
    earlier = (iota((64, 64), 0) // R == iota((64, 64), 1) // R) & (iota((64, 64), 1) < iota((64, 64), 0))
    rank = dot(jnp.where(earlier, 1.0, 0.0).astype(BF16), named.astype(BF16))
    gather = jnp.where(
        (named > 0.5) & (rank.astype(jnp.int32) == lax.rem(cols // 8, 2)) & (lax.rem(cols, 8) == rows // R), 1.0, 0.0
    ).astype(BF16)
    rows, cols = iota((64, 64), 0), iota((64, 64), 1)
    swap = jnp.where((rows // 8 == lax.rem(cols, 8)) & (lax.rem(rows, 8) == cols // 8), 1.0, 0.0).astype(BF16)

    own_states = st_v[:, pl.ds(pl.multiple_of(chunk * 256, 256), 256)].astype(F32)
    arrived(0, recv1.at[pl.ds(0, NZ - 1)])
    residual_chunk = (own_states + jnp.sum(recv1[...].astype(F32), axis=0)).astype(BF16)
    rz[chunk] = residual_chunk

    to_near_mp(lambda k: remote(1, rz.at[chunk], rz.at[chunk], (g, d, k)))
    arrived(1, rz.at[pl.ds(0, NC - 1)])
    pieces = [rz[q].astype(F32) for q in range(NC)]
    squares = sum(jnp.sum(p * p, axis=1, keepdims=True) for p in pieces)
    inv = lax.rsqrt(squares / D + EPSILON)
    stacked = jnp.concatenate([p * inv for p in pieces], axis=0).astype(BF16)

    send3[...] = dot(scatter, stacked).astype(BF16).reshape(NP, 16, 256)

    to_plane(lambda p, q: remote(2, send3.at[p * ND + q], recv3.at[me], (p, q, m)))
    recv3[me] = send3[me]
    for name in ("ein0", "ein1", "eout"):
        loads[name].wait()
    arrived(2, recv3.at[pl.ds(0, NP - 1)])
    tokens = []
    for n in range(8):
        turned = dot(swap, recv3[4 * n : 4 * n + 4].reshape(64, 256))
        tokens.append(jnp.concatenate([turned[8 * q : 8 * q + 8] for q in range(8)], axis=1))
    tokens = jnp.concatenate(tokens, axis=0).astype(BF16)
    both = dot(tokens, ein_v[...])
    gate, upward = both[:, :HD], both[:, HD:]
    activated = (gate / (1.0 + jnp.exp(-gate)) * upward * coefficient).astype(BF16)
    terms = dot(activated, eout_v[...])
    for n in range(8):
        part = terms[8 * n : 8 * n + 8]
        part = jnp.concatenate([part[:, 256 * q : 256 * q + 256] for q in range(8)], axis=0).astype(BF16)
        send4[4 * n : 4 * n + 4] = dot(swap, part).astype(BF16).reshape(4, 16, 256)

    to_plane(lambda p, q: remote(3, send4.at[p * ND + q], recv4.at[me], (p, q, m)))
    recv4[me] = send4[me]
    arrived(3, recv4.at[pl.ds(0, NP - 1)])
    own_terms = dot(gather, recv4[...].reshape(512, 256))
    for j in range(NC):
        send5[j] = own_terms[8 * j : 8 * j + 8].astype(BF16)

    to_mp(lambda k: remote(4, send5.at[lax.rem(k, NC)], recv5.at[m], (g, d, k)))
    recv5[m] = send5[chunk]
    arrived(4, recv5.at[pl.ds(0, NZ - 1)])
    uz[chunk] = (residual_chunk.astype(F32) + jnp.sum(recv5[...].astype(F32), axis=0)).astype(BF16)

    to_near_mp(lambda k: remote(5, uz.at[chunk], uz.at[chunk], (g, d, k)))
    loads["guid"].wait()
    guidance = column(gd_v[...])
    share = jnp.where(g == 0, guidance, 1.0 - guidance)
    low = iota((R, HD), 1) < 64
    arrived(5, uz.at[pl.ds(0, NC - 1)])
    pieces = [uz[j].astype(F32) for j in range(NC)]
    squares = sum(jnp.sum(p * p, axis=1, keepdims=True) for p in pieces)
    inv = lax.rsqrt(squares / D + EPSILON)
    finals = [(p * inv).astype(BF16).astype(F32) * share for p in pieces]
    finals = [finals[j // 2][:, j % 2 * HD : j % 2 * HD + HD] for j in range(NZ)]
    for j in range(NC):
        first, second = finals[j], finals[j + NC]
        send7[2 * j] = jnp.where(low, first, pltpu.roll(second, 64, axis=1))
        send7[2 * j + 1] = jnp.where(low, pltpu.roll(first, 64, axis=1), second)

    to_plane(lambda p, q: remote(6, send7.at[q], recv7.at[me], (p, q, m)))
    recv7[me] = send7[d]
    loads["vocab"].wait()
    arrived(8, voc_v.at[pl.ds(0, 64), :])
    arrived(6, recv7.at[pl.ds(0, NP - 1)])
    mixed = (recv7[:ND] + recv7[ND:]).reshape(ND * R, HD).astype(BF16)
    send8[...] = dot(mixed, voc_v[...]).reshape(ND, R, WIDE).astype(BF16)

    to_chips(lambda p, q: remote(7, send8.at[q], recv8.at[d], (p, q, m)))
    recv8[d] = send8[d]
    arrived(7, recv8.at[pl.ds(0, ND - 1)])
    logits = jnp.sum(recv8[...].astype(F32), axis=0)
    logits = jnp.where(g == 0, logits, pltpu.roll(logits, WIDE - 64, axis=1))
    for r in range(R):
        out_ref[r] = logits[r : r + 1, :HALF]

    sent(0, recv1.at[pl.ds(0, NZ - 1)])
    sent(1, rz.at[pl.ds(0, NC - 1)])
    sent(2, recv3.at[pl.ds(0, NP - 1)])
    sent(3, recv4.at[pl.ds(0, NP - 1)])
    sent(4, recv5.at[pl.ds(0, NZ - 1)])
    sent(5, uz.at[pl.ds(0, NC - 1)])
    sent(6, recv7.at[pl.ds(0, NP - 1)])
    sent(7, recv8.at[pl.ds(0, ND - 1)])
    sent(8, voc_v.at[pl.ds(0, 64), :])


def body(
    states, lengths, sink_cache, window_cache, qkv_weight, out_weight, expert_ids, route_weight,
    expert_in, expert_out, vocab_weight, guidance,
):
    qkv = jnp.transpose(qkv_weight, (1, 2, 0, 3)).reshape(3, D, HD)
    ids = jnp.transpose(expert_ids, (0, 2, 1))
    route = jnp.transpose(route_weight, (0, 2, 1))
    guided = pl.pallas_call(
        kernel,
        out_shape=jax.ShapeDtypeStruct((R, 1, HALF), F32),
        in_specs=[pl.BlockSpec(memory_space=pl.ANY)] * 12,
        out_specs=pl.BlockSpec(memory_space=pltpu.VMEM),
        scratch_shapes=[
            pltpu.VMEM((R, D), BF16),
            pltpu.VMEM((1, R), jnp.int32),
            pltpu.VMEM((R, 2, SINKS, HD), BF16),
            pltpu.VMEM((2 * R * SINKS, HD), F32),
            pltpu.VMEM((R, WINDOW, HD), BF16),
            pltpu.VMEM((R, WINDOW, HD), BF16),
            pltpu.VMEM((D, 3 * HD), BF16),
            pltpu.VMEM((HD, D), BF16),
            pltpu.VMEM((2, 8, HD), jnp.int32),
            pltpu.VMEM((2, 8, HD), F32),
            pltpu.VMEM((D, 2 * HD), BF16),
            pltpu.VMEM((HD, D), BF16),
            pltpu.VMEM((HD, WIDE), BF16),
            pltpu.VMEM((1, R), F32),
            pltpu.VMEM((NC, R, 256), BF16),
            pltpu.VMEM((NZ, R, 256), BF16),
            pltpu.VMEM((NC, R, 256), BF16),
            pltpu.VMEM((NP, 16, 256), BF16),
            pltpu.VMEM((NP, 16, 256), BF16),
            pltpu.VMEM((NP, 16, 256), BF16),
            pltpu.VMEM((NP, 16, 256), BF16),
            pltpu.VMEM((NC, R, 256), BF16),
            pltpu.VMEM((NZ, R, 256), BF16),
            pltpu.VMEM((NC, R, 256), BF16),
            pltpu.VMEM((ND, R, HD), F32),
            pltpu.VMEM((NP, R, HD), F32),
            pltpu.VMEM((ND, R, WIDE), BF16),
            pltpu.VMEM((ND, R, WIDE), BF16),
            pltpu.SemaphoreType.DMA((16,)),
            pltpu.SemaphoreType.DMA((9,)),
            pltpu.SemaphoreType.DMA((9,)),
        ],
        compiler_params=pltpu.CompilerParams(
            collective_id=0, has_side_effects=True, vmem_limit_bytes=56 << 20
        ),
    )(
        states, lengths, sink_cache, window_cache, qkv, out_weight, ids, route,
        expert_in, expert_out, vocab_weight, guidance.reshape(1, R),
    )
    return guided.reshape(R, 1, 1, HALF)


def solution(mesh):
    in_specs = (
        P("guide", "dp", None),
        P("guide", "dp"),
        P("guide", "dp", "mp", None, None, None),
        P("guide", "dp", "mp", None, None, None),
        P(None, None, "mp", None),
        P("mp", None, None),
        P(),
        P(),
        P(None, None, ("guide", "dp", "mp")),
        P(("guide", "dp", "mp"), None),
        P(("guide", "dp"), "mp"),
        P("dp"),
    )
    out_specs = P("dp", "mp", "guide", None)
    return jax.shard_map(body, mesh=mesh, in_specs=in_specs, out_specs=out_specs, check_vma=False)
```

```python
import math

import jax
import jax.numpy as jnp
from jax import lax
from jax.experimental import pallas as pl
from jax.experimental.pallas import tpu as pltpu
from jax.sharding import PartitionSpec as P

F32 = jnp.float32
BF16 = jnp.bfloat16
EPSILON = 1e-05
MESH = pl.DeviceIdType.MESH
D = 2048
HD = 128
R = 8
NZ = 16
ND = 16
NP = 32
NC = 8
SINKS = 4
WINDOW = 256
HALF = 832
WIDE = 896
NEG = -1e30


def iota(shape, axis):
    return lax.broadcasted_iota(jnp.int32, shape, axis)


def dot(a, b):
    return jnp.dot(a, b, preferred_element_type=F32)


def dot_nt(a, b):
    return lax.dot_general(a, b, (((1,), (1,)), ((), ())), preferred_element_type=F32)


def column(row):
    square = jnp.broadcast_to(row, (R, R))
    return jnp.sum(jnp.where(iota((R, R), 0) == iota((R, R), 1), square, 0.0), axis=1, keepdims=True)


def kernel(
    states_h, lengths_h, sink_h, window_h, qkv_h, outw_h, ids_h, route_h, ein_h, eout_h, vocab_h, guid_h,
    out_ref,
    st_v, len_v, sink_v, sinkf_v, k_v, v_v, qkv_v, outw_v, ids_v, rw_v, ein_v, eout_v, voc_v, gd_v,
    send1, recv1, windows, rz, gsend, grecv, send3, recv3, send4, recv4, send5, recv5, uz, send7, recv7, send8, recv8,
    local_sem, send_sem, recv_sem,
):
    g = lax.axis_index("guide")
    d = lax.axis_index("dp")
    m = lax.axis_index("mp")
    me = g * ND + d

    barrier = pltpu.get_barrier_semaphore()

    y, x = d // 4, lax.rem(d, 4)

    def turn(a):
        return jnp.where(a == 0, 2, jnp.where(a == 1, 1, jnp.where(a == 2, 3, 0)))

    def chip(i):
        return lax.rem(y + turn(i // 4), 4) * 4 + lax.rem(x + turn(lax.rem(i, 4)), 4)

    def to_chips(act):
        def step(i, carry):
            other = chip(i)
            act(g, other)
            return carry

        lax.fori_loop(0, ND - 1, step, 0)

    def to_plane(act):
        def step(i, carry):
            other = chip(i)
            act(0, other)
            act(1, other)
            return carry

        lax.fori_loop(0, ND - 1, step, 0)
        act(1 - g, d)

    def to_mp(act):
        def step(i, carry):
            offset = jnp.where(lax.rem(i, 2) == 0, 8 + i // 2, 8 - (i + 1) // 2)
            act(lax.rem(m + offset, NZ))
            return carry

        lax.fori_loop(0, NZ - 1, step, 0)

    def to_near_mp(act):
        def step(i, carry):
            offset = jnp.where(lax.rem(i, 2) == 0, 4 - i // 2, 13 + i // 2)
            act(lax.rem(m + offset, NZ))
            return carry

        lax.fori_loop(0, NC - 1, step, 0)

    def greet(device):
        pl.semaphore_signal(barrier, inc=1, device_id=device, device_id_type=MESH)

    to_near_mp(lambda k: greet((g, d, k)))
    greet((g, d, lax.rem(m + 12, NZ)))
    to_plane(lambda p, q: greet((p, q, m)))

    loads = {}

    def load(name, src, dst):
        copy = pltpu.make_async_copy(src, dst, local_sem.at[len(loads)])
        loads[name] = copy
        copy.start()

    load("states", states_h.at[0], st_v)
    load("lengths", lengths_h, len_v)
    for t in range(3):
        load("qkv%d" % t, qkv_h.at[t], qkv_v.at[:, pl.ds(t * HD, HD)])
    load("sink", sink_h.at[0, :, 0], sink_v)
    load("k", window_h.at[0, :, 0, 0], k_v)
    load("v", window_h.at[0, :, 0, 1], v_v)
    load("outw", outw_h.at[0], outw_v)
    load("ids", ids_h, ids_v)
    load("route", route_h, rw_v)
    load("ein0", ein_h.at[0], ein_v.at[:, pl.ds(0, HD)])
    load("ein1", ein_h.at[1], ein_v.at[:, pl.ds(HD, HD)])
    load("eout", eout_h, eout_v)
    own_columns = pl.ds(pl.multiple_of(g * 768, HD), WIDE)
    own_rows = pl.ds(pl.multiple_of(g * 64, 64), 64)
    load("vocab", vocab_h.at[:, own_columns], voc_v.at[own_rows, :])
    load("guid", guid_h, gd_v)

    def remote(phase, src, dst, device):
        pltpu.make_async_remote_copy(
            src_ref=src, dst_ref=dst, send_sem=send_sem.at[phase], recv_sem=recv_sem.at[phase],
            device_id=device, device_id_type=MESH,
        ).start()

    def arrived(phase, ref):
        pltpu.make_async_copy(ref, ref, recv_sem.at[phase]).wait()

    def sent(phase, ref):
        pltpu.make_async_copy(ref, ref, send_sem.at[phase]).wait()

    step_index = lax.rem(iota((1, HD), 1), HD // 2).astype(F32)
    inverse = jnp.exp(step_index * (-2.0 * math.log(10000.0) / HD))
    loads["lengths"].wait()
    position = column(len_v[...].astype(F32))
    angles = position * inverse
    cosine = jnp.cos(angles)
    sine = jnp.sin(angles)
    sine = jnp.where(iota((R, HD), 1) < HD // 2, -sine, sine)
    loads["states"].wait()
    hidden = st_v[...].astype(F32)
    normed = (hidden * lax.rsqrt(jnp.mean(hidden * hidden, axis=-1, keepdims=True) + EPSILON)).astype(BF16)
    loads["sink"].wait()
    for r in range(R):
        for t in range(2):
            sinkf_v[pl.ds(t * R * SINKS + r * SINKS, SINKS), :] = sink_v[r, t].astype(F32)
    for t in range(3):
        loads["qkv%d" % t].wait()
    projected = dot(normed, qkv_v[...])
    query = projected[:, :HD]
    key = projected[:, HD : 2 * HD]
    query = (query * cosine + pltpu.roll(query, HD // 2, axis=1) * sine).astype(BF16)
    key = (key * cosine + pltpu.roll(key, HD // 2, axis=1) * sine).astype(BF16)
    fresh = projected[:, 2 * HD :].astype(BF16)
    root = 1.0 / math.sqrt(HD)
    sinks = sinkf_v[...].astype(BF16)
    loads["k"].wait()
    window_scores = dot_nt(query, k_v[...].reshape(R * WINDOW, HD)) * root
    sink_scores = dot_nt(query, sinks[: R * SINKS]) * root
    self_scores = jnp.sum(query.astype(F32) * key.astype(F32), axis=1, keepdims=True) * root
    position_i = position.astype(jnp.int32)
    slot = iota((R, R * WINDOW), 1)
    window_ok = (slot // WINDOW == iota((R, R * WINDOW), 0)) & (
        lax.rem(slot, WINDOW) >= SINKS + WINDOW - position_i
    )
    slot = iota((R, R * SINKS), 1)
    sink_ok = (slot // SINKS == iota((R, R * SINKS), 0)) & (lax.rem(slot, SINKS) < position_i)
    window_scores = jnp.where(window_ok, window_scores, NEG)
    sink_scores = jnp.where(sink_ok, sink_scores, NEG)
    highest = jnp.maximum(
        jnp.maximum(
            jnp.max(window_scores, axis=1, keepdims=True), jnp.max(sink_scores, axis=1, keepdims=True)
        ),
        self_scores,
    )
    window_exp = jnp.where(window_ok, jnp.exp(window_scores - highest), 0.0)
    sink_exp = jnp.where(sink_ok, jnp.exp(sink_scores - highest), 0.0)
    self_exp = jnp.exp(self_scores - highest)
    total = jnp.sum(window_exp, axis=1, keepdims=True) + jnp.sum(sink_exp, axis=1, keepdims=True) + self_exp
    scale = 1.0 / total
    window_prob = (window_exp * scale).astype(BF16)
    sink_prob = (sink_exp * scale).astype(BF16)
    self_prob = (self_exp * scale).astype(BF16).astype(F32)
    loads["v"].wait()
    mixture = (
        dot(window_prob, v_v[...].reshape(R * WINDOW, HD))
        + dot(sink_prob, sinks[R * SINKS :])
        + self_prob * fresh.astype(F32)
    ).astype(BF16)
    loads["outw"].wait()
    partial = dot(mixture, outw_v[...])
    for j in range(NC):
        send1[j] = partial[:, j * 256 : (j + 1) * 256].astype(BF16)
    chunk = lax.rem(m, NC)

    pl.semaphore_wait(barrier, NC + NP - 1)

    to_near_mp(lambda k: remote(0, send1.at[lax.rem(k, NC)], recv1.at[chunk], (g, d, k)))
    recv1[chunk] = send1[chunk]
    remote(8, vocab_h.at[:, pl.ds(pl.multiple_of((1 - g) * 768, HD), WIDE)], voc_v.at[own_rows, :], (1 - g, d, m))

    loads["guid"].wait()
    gsend[...] = jnp.broadcast_to(column(gd_v[...]), (R, HD))
    to_chips(lambda p, q: remote(9, gsend, grecv.at[d], (p, q, m)))
    grecv[d] = gsend[...]

    loads["ids"].wait()
    loads["route"].wait()
    half = m // (NZ // 2)
    own_expert = 2 * me + half
    before = (iota((HD, HD), 0) // R == iota((HD, HD), 1) // R) & (iota((HD, HD), 0) < iota((HD, HD), 1))
    before = jnp.where(before, 1.0, 0.0).astype(BF16)
    coefficients = []
    for s in range(2):
        match = ids_v[s] == own_expert
        chosen = jnp.sum(jnp.where(match, 1.0, 0.0), axis=0, keepdims=True)
        weight = jnp.sum(jnp.where(match, rw_v[s], 0.0), axis=0, keepdims=True)
        rank = dot(jnp.broadcast_to(chosen, (R, HD)).astype(BF16), before)[:1]
        rows, lanes = iota((32, HD), 0), iota((32, HD), 1)
        takes = (lanes // R == rows // 2) & (rank.astype(jnp.int32) == lax.rem(rows, 2)) & (chosen > 0.5)
        coefficients.append(jnp.sum(jnp.where(takes, weight, 0.0), axis=1, keepdims=True))
    coefficient = jnp.concatenate(coefficients, axis=0)

    own_ids = jnp.where(g == 0, ids_v[0], ids_v[1]).astype(F32).astype(BF16)
    pick = jnp.where(iota((HD, 64), 0) == d * R + lax.rem(iota((HD, 64), 1), R), 1.0, 0.0).astype(BF16)
    ids_row = dot(own_ids, pick)
    pick = jnp.where(iota((64, HD), 1) == d * R + lax.rem(iota((64, HD), 0), R), 1.0, 0.0).astype(BF16)
    ids_col = dot_nt(pick, own_ids)
    rows = iota((512, 64), 0)
    cols = iota((512, 64), 1)
    expert = (rows // 16 * 2 + half).astype(F32)
    named = jnp.zeros((512, 64), F32)
    for i in range(8):
        named = jnp.where(expert == ids_row[i : i + 1, :], 1.0, named)
    earlier = (iota((64, 64), 0) // R == iota((64, 64), 1) // R) & (iota((64, 64), 0) < iota((64, 64), 1))
    rank = dot(named.astype(BF16), jnp.where(earlier, 1.0, 0.0).astype(BF16))
    scatter = jnp.where(
        (named > 0.5) & (rank.astype(jnp.int32) == lax.rem(rows // 8, 2)) & (lax.rem(rows, 8) == cols // R), 1.0, 0.0
    ).astype(BF16)
    rows = iota((64, 512), 0)
    cols = iota((64, 512), 1)
    expert = (cols // 16 * 2 + half).astype(F32)
    named = jnp.zeros((64, 512), F32)
    for i in range(8):
        named = jnp.where(expert == ids_col[:, i : i + 1], 1.0, named)
    earlier = (iota((64, 64), 0) // R == iota((64, 64), 1) // R) & (iota((64, 64), 1) < iota((64, 64), 0))
    rank = dot(jnp.where(earlier, 1.0, 0.0).astype(BF16), named.astype(BF16))
    gather = jnp.where(
        (named > 0.5) & (rank.astype(jnp.int32) == lax.rem(cols // 8, 2)) & (lax.rem(cols, 8) == rows // R), 1.0, 0.0
    ).astype(BF16)
    rows, cols = iota((64, 64), 0), iota((64, 64), 1)
    swap = jnp.where((rows // 8 == lax.rem(cols, 8)) & (lax.rem(rows, 8) == cols // 8), 1.0, 0.0).astype(BF16)

    arrived(0, recv1.at[pl.ds(0, NC - 1)])
    windows[m] = jnp.sum(recv1[...].astype(F32), axis=0).astype(BF16)

    to_mp(lambda k: remote(1, windows.at[m], windows.at[m], (g, d, k)))
    arrived(1, windows.at[pl.ds(0, NZ - 1)])
    pieces = []
    for q in range(NC):
        total = windows[q].astype(F32) + windows[q + NC].astype(F32)
        rz[q] = (st_v[:, q * 256 : q * 256 + 256].astype(F32) + total).astype(BF16)
        pieces.append(rz[q].astype(F32))
    squares = sum(jnp.sum(p * p, axis=1, keepdims=True) for p in pieces)
    inv = lax.rsqrt(squares / D + EPSILON)
    stacked = jnp.concatenate([p * inv for p in pieces], axis=0).astype(BF16)

    send3[...] = dot(scatter, stacked).astype(BF16).reshape(NP, 16, 256)

    to_plane(lambda p, q: remote(2, send3.at[p * ND + q], recv3.at[me], (p, q, m)))
    recv3[me] = send3[me]
    for name in ("ein0", "ein1", "eout"):
        loads[name].wait()
    arrived(2, recv3.at[pl.ds(0, NP - 1)])
    tokens = []
    for n in range(8):
        turned = dot(swap, recv3[4 * n : 4 * n + 4].reshape(64, 256))
        tokens.append(jnp.concatenate([turned[8 * q : 8 * q + 8] for q in range(8)], axis=1))
    tokens = jnp.concatenate(tokens, axis=0).astype(BF16)
    both = dot(tokens, ein_v[...])
    gate, upward = both[:, :HD], both[:, HD:]
    activated = (gate / (1.0 + jnp.exp(-gate)) * upward * coefficient).astype(BF16)
    terms = dot(activated, eout_v[...])
    for n in range(8):
        part = terms[8 * n : 8 * n + 8]
        part = jnp.concatenate([part[:, 256 * q : 256 * q + 256] for q in range(8)], axis=0).astype(BF16)
        send4[4 * n : 4 * n + 4] = dot(swap, part).astype(BF16).reshape(4, 16, 256)

    to_plane(lambda p, q: remote(3, send4.at[p * ND + q], recv4.at[me], (p, q, m)))
    recv4[me] = send4[me]
    arrived(3, recv4.at[pl.ds(0, NP - 1)])
    own_terms = dot(gather, recv4[...].reshape(512, 256))
    for j in range(NC):
        send5[j] = own_terms[8 * j : 8 * j + 8].astype(BF16)

    to_mp(lambda k: remote(4, send5.at[lax.rem(k, NC)], recv5.at[m], (g, d, k)))
    recv5[m] = send5[chunk]
    arrived(4, recv5.at[pl.ds(0, NZ - 1)])
    uz[chunk] = (rz[chunk].astype(F32) + jnp.sum(recv5[...].astype(F32), axis=0)).astype(BF16)

    to_near_mp(lambda k: remote(5, uz.at[chunk], uz.at[chunk], (g, d, k)))
    low = iota((R, HD), 1) < 64
    arrived(5, uz.at[pl.ds(0, NC - 1)])
    pieces = [uz[j].astype(F32) for j in range(NC)]
    squares = sum(jnp.sum(p * p, axis=1, keepdims=True) for p in pieces)
    inv = lax.rsqrt(squares / D + EPSILON)
    finals = [p * inv for p in pieces]
    finals = [finals[j // 2][:, j % 2 * HD : j % 2 * HD + HD] for j in range(NZ)]
    for j in range(NC):
        first, second = finals[j], finals[j + NC]
        send7[2 * j] = jnp.where(low, first, pltpu.roll(second, 64, axis=1)).astype(BF16)
        send7[2 * j + 1] = jnp.where(low, pltpu.roll(first, 64, axis=1), second).astype(BF16)

    to_plane(lambda p, q: remote(6, send7.at[q], recv7.at[me], (p, q, m)))
    recv7[me] = send7[d]
    loads["vocab"].wait()
    arrived(8, voc_v.at[pl.ds(0, 64), :])
    arrived(6, recv7.at[pl.ds(0, NP - 1)])
    arrived(9, grecv.at[pl.ds(0, ND - 1)])
    conditional, unconditional = recv7[:ND].astype(F32), recv7[ND:].astype(F32)
    mixed = unconditional + grecv[...] * (conditional - unconditional)
    mixed = mixed.reshape(ND * R, HD).astype(BF16)
    send8[...] = dot(mixed, voc_v[...]).reshape(ND, R, WIDE).astype(BF16)

    to_chips(lambda p, q: remote(7, send8.at[q], recv8.at[d], (p, q, m)))
    recv8[d] = send8[d]
    arrived(7, recv8.at[pl.ds(0, ND - 1)])
    logits = jnp.sum(recv8[...].astype(F32), axis=0)
    logits = jnp.where(g == 0, logits, pltpu.roll(logits, WIDE - 64, axis=1))
    for r in range(R):
        out_ref[r] = logits[r : r + 1, :HALF]

    sent(0, recv1.at[pl.ds(0, NC - 1)])
    sent(1, windows.at[pl.ds(0, NZ - 1)])
    sent(2, recv3.at[pl.ds(0, NP - 1)])
    sent(3, recv4.at[pl.ds(0, NP - 1)])
    sent(4, recv5.at[pl.ds(0, NZ - 1)])
    sent(5, uz.at[pl.ds(0, NC - 1)])
    sent(6, recv7.at[pl.ds(0, NP - 1)])
    sent(7, recv8.at[pl.ds(0, ND - 1)])
    sent(8, voc_v.at[pl.ds(0, 64), :])
    sent(9, grecv.at[pl.ds(0, ND - 1)])


def body(
    states, lengths, sink_cache, window_cache, qkv_weight, out_weight, expert_ids, route_weight,
    expert_in, expert_out, vocab_weight, guidance,
):
    qkv = jnp.transpose(qkv_weight, (1, 2, 0, 3)).reshape(3, D, HD)
    ids = jnp.transpose(expert_ids, (0, 2, 1))
    route = jnp.transpose(route_weight, (0, 2, 1))
    guided = pl.pallas_call(
        kernel,
        out_shape=jax.ShapeDtypeStruct((R, 1, HALF), F32),
        in_specs=[pl.BlockSpec(memory_space=pl.ANY)] * 12,
        out_specs=pl.BlockSpec(memory_space=pltpu.VMEM),
        scratch_shapes=[
            pltpu.VMEM((R, D), BF16),
            pltpu.VMEM((1, R), jnp.int32),
            pltpu.VMEM((R, 2, SINKS, HD), BF16),
            pltpu.VMEM((2 * R * SINKS, HD), F32),
            pltpu.VMEM((R, WINDOW, HD), BF16),
            pltpu.VMEM((R, WINDOW, HD), BF16),
            pltpu.VMEM((D, 3 * HD), BF16),
            pltpu.VMEM((HD, D), BF16),
            pltpu.VMEM((2, 8, HD), jnp.int32),
            pltpu.VMEM((2, 8, HD), F32),
            pltpu.VMEM((D, 2 * HD), BF16),
            pltpu.VMEM((HD, D), BF16),
            pltpu.VMEM((HD, WIDE), BF16),
            pltpu.VMEM((1, R), F32),
            pltpu.VMEM((NC, R, 256), BF16),
            pltpu.VMEM((NC, R, 256), BF16),
            pltpu.VMEM((NZ, R, 256), BF16),
            pltpu.VMEM((NC, R, 256), BF16),
            pltpu.VMEM((R, HD), F32),
            pltpu.VMEM((ND, R, HD), F32),
            pltpu.VMEM((NP, 16, 256), BF16),
            pltpu.VMEM((NP, 16, 256), BF16),
            pltpu.VMEM((NP, 16, 256), BF16),
            pltpu.VMEM((NP, 16, 256), BF16),
            pltpu.VMEM((NC, R, 256), BF16),
            pltpu.VMEM((NZ, R, 256), BF16),
            pltpu.VMEM((NC, R, 256), BF16),
            pltpu.VMEM((ND, R, HD), BF16),
            pltpu.VMEM((NP, R, HD), BF16),
            pltpu.VMEM((ND, R, WIDE), BF16),
            pltpu.VMEM((ND, R, WIDE), BF16),
            pltpu.SemaphoreType.DMA((16,)),
            pltpu.SemaphoreType.DMA((10,)),
            pltpu.SemaphoreType.DMA((10,)),
        ],
        compiler_params=pltpu.CompilerParams(
            collective_id=0, has_side_effects=True, vmem_limit_bytes=56 << 20
        ),
    )(
        states, lengths, sink_cache, window_cache, qkv, out_weight, ids, route,
        expert_in, expert_out, vocab_weight, guidance.reshape(1, R),
    )
    return guided.reshape(R, 1, 1, HALF)


def solution(mesh):
    in_specs = (
        P("guide", "dp", None),
        P("guide", "dp"),
        P("guide", "dp", "mp", None, None, None),
        P("guide", "dp", "mp", None, None, None),
        P(None, None, "mp", None),
        P("mp", None, None),
        P(),
        P(),
        P(None, None, ("guide", "dp", "mp")),
        P(("guide", "dp", "mp"), None),
        P(("guide", "dp"), "mp"),
        P("dp"),
    )
    out_specs = P("dp", "mp", "guide", None)
    return jax.shard_map(body, mesh=mesh, in_specs=in_specs, out_specs=out_specs, check_vma=False)
```

```python
import math

import jax
import jax.numpy as jnp
from jax import lax
from jax.experimental import pallas as pl
from jax.experimental.pallas import tpu as pltpu
from jax.sharding import PartitionSpec as P

F32 = jnp.float32
BF16 = jnp.bfloat16
EPSILON = 1e-05
MESH = pl.DeviceIdType.MESH
D = 2048
HD = 128
R = 8
NZ = 16
ND = 16
NP = 32
NC = 8
SINKS = 4
WINDOW = 256
HALF = 832
WIDE = 896
NEG = -1e30


def iota(shape, axis):
    return lax.broadcasted_iota(jnp.int32, shape, axis)


def dot(a, b):
    return jnp.dot(a, b, preferred_element_type=F32)


def dot_nt(a, b):
    return lax.dot_general(a, b, (((1,), (1,)), ((), ())), preferred_element_type=F32)


def column(row):
    square = jnp.broadcast_to(row, (R, R))
    return jnp.sum(jnp.where(iota((R, R), 0) == iota((R, R), 1), square, 0.0), axis=1, keepdims=True)


def kernel(
    states_h, lengths_h, sink_h, window_h, qkv_h, outw_h, ids_h, route_h, ein_h, eout_h, vocab_h, guid_h,
    out_ref,
    st_v, len_v, sink_v, sinkf_v, k_v, v_v, qkv_v, outw_v, ids_v, rw_v, ein_v, eout_v, voc_v, gd_v,
    send1, recv1, windows, gather, rsend, rrecv, send3, recv3, send4, recv4, send5, recv5, uz, send8, recv8,
    local_sem, send_sem, recv_sem,
):
    g = lax.axis_index("guide")
    d = lax.axis_index("dp")
    m = lax.axis_index("mp")
    me = g * ND + d

    barrier = pltpu.get_barrier_semaphore()

    y, x = d // 4, lax.rem(d, 4)

    def turn(a):
        return jnp.where(a == 0, 2, jnp.where(a == 1, 1, jnp.where(a == 2, 3, 0)))

    def chip(i):
        return lax.rem(y + turn(i // 4), 4) * 4 + lax.rem(x + turn(lax.rem(i, 4)), 4)

    def to_chips(act):
        def step(i, carry):
            other = chip(i)
            act(g, other)
            return carry

        lax.fori_loop(0, ND - 1, step, 0)

    def to_plane(act):
        def step(i, carry):
            other = chip(i)
            act(0, other)
            act(1, other)
            return carry

        lax.fori_loop(0, ND - 1, step, 0)
        act(1 - g, d)

    def to_mp(act):
        def step(i, carry):
            offset = jnp.where(lax.rem(i, 2) == 0, 8 + i // 2, 8 - (i + 1) // 2)
            act(lax.rem(m + offset, NZ))
            return carry

        lax.fori_loop(0, NZ - 1, step, 0)

    def to_near_mp(act):
        def step(i, carry):
            offset = jnp.where(lax.rem(i, 2) == 0, 4 - i // 2, 13 + i // 2)
            act(lax.rem(m + offset, NZ))
            return carry

        lax.fori_loop(0, NC - 1, step, 0)

    def greet(device):
        pl.semaphore_signal(barrier, inc=1, device_id=device, device_id_type=MESH)

    to_near_mp(lambda k: greet((g, d, k)))
    greet((g, d, lax.rem(m + 12, NZ)))
    to_plane(lambda p, q: greet((p, q, m)))

    loads = {}

    def load(name, src, dst):
        copy = pltpu.make_async_copy(src, dst, local_sem.at[len(loads)])
        loads[name] = copy
        copy.start()

    load("states", states_h.at[0], st_v)
    load("lengths", lengths_h, len_v)
    for t in range(3):
        load("qkv%d" % t, qkv_h.at[t], qkv_v.at[:, pl.ds(t * HD, HD)])
    load("sink", sink_h.at[0, :, 0], sink_v)
    load("k", window_h.at[0, :, 0, 0], k_v)
    load("v", window_h.at[0, :, 0, 1], v_v)
    load("outw", outw_h.at[0], outw_v)
    load("ids", ids_h, ids_v)
    load("route", route_h, rw_v)
    load("ein0", ein_h.at[0], ein_v.at[:, pl.ds(0, HD)])
    load("ein1", ein_h.at[1], ein_v.at[:, pl.ds(HD, HD)])
    load("eout", eout_h, eout_v)
    own_columns = pl.ds(pl.multiple_of(g * 768, HD), WIDE)
    own_rows = pl.ds(pl.multiple_of(g * 64, 64), 64)
    load("vocab", vocab_h.at[:, own_columns], voc_v.at[own_rows, :])
    load("guid", guid_h, gd_v)

    def remote(phase, src, dst, device):
        pltpu.make_async_remote_copy(
            src_ref=src, dst_ref=dst, send_sem=send_sem.at[phase], recv_sem=recv_sem.at[phase],
            device_id=device, device_id_type=MESH,
        ).start()

    def arrived(phase, ref):
        pltpu.make_async_copy(ref, ref, recv_sem.at[phase]).wait()

    def sent(phase, ref):
        pltpu.make_async_copy(ref, ref, send_sem.at[phase]).wait()

    step_index = lax.rem(iota((1, HD), 1), HD // 2).astype(F32)
    inverse = jnp.exp(step_index * (-2.0 * math.log(10000.0) / HD))
    loads["lengths"].wait()
    position = column(len_v[...].astype(F32))
    angles = position * inverse
    cosine = jnp.cos(angles)
    sine = jnp.sin(angles)
    sine = jnp.where(iota((R, HD), 1) < HD // 2, -sine, sine)
    loads["states"].wait()
    hidden = st_v[...].astype(F32)
    normed = (hidden * lax.rsqrt(jnp.mean(hidden * hidden, axis=-1, keepdims=True) + EPSILON)).astype(BF16)
    loads["sink"].wait()
    for r in range(R):
        for t in range(2):
            sinkf_v[pl.ds(t * R * SINKS + r * SINKS, SINKS), :] = sink_v[r, t].astype(F32)
    for t in range(3):
        loads["qkv%d" % t].wait()
    projected = dot(normed, qkv_v[...])
    query = projected[:, :HD]
    key = projected[:, HD : 2 * HD]
    query = (query * cosine + pltpu.roll(query, HD // 2, axis=1) * sine).astype(BF16)
    key = (key * cosine + pltpu.roll(key, HD // 2, axis=1) * sine).astype(BF16)
    fresh = projected[:, 2 * HD :].astype(BF16)
    root = 1.0 / math.sqrt(HD)
    sinks = sinkf_v[...].astype(BF16)
    loads["k"].wait()
    window_scores = dot_nt(query, k_v[...].reshape(R * WINDOW, HD)) * root
    sink_scores = dot_nt(query, sinks[: R * SINKS]) * root
    self_scores = jnp.sum(query.astype(F32) * key.astype(F32), axis=1, keepdims=True) * root
    position_i = position.astype(jnp.int32)
    slot = iota((R, R * WINDOW), 1)
    window_ok = (slot // WINDOW == iota((R, R * WINDOW), 0)) & (
        lax.rem(slot, WINDOW) >= SINKS + WINDOW - position_i
    )
    slot = iota((R, R * SINKS), 1)
    sink_ok = (slot // SINKS == iota((R, R * SINKS), 0)) & (lax.rem(slot, SINKS) < position_i)
    window_scores = jnp.where(window_ok, window_scores, NEG)
    sink_scores = jnp.where(sink_ok, sink_scores, NEG)
    highest = jnp.maximum(
        jnp.maximum(
            jnp.max(window_scores, axis=1, keepdims=True), jnp.max(sink_scores, axis=1, keepdims=True)
        ),
        self_scores,
    )
    window_exp = jnp.where(window_ok, jnp.exp(window_scores - highest), 0.0)
    sink_exp = jnp.where(sink_ok, jnp.exp(sink_scores - highest), 0.0)
    self_exp = jnp.exp(self_scores - highest)
    total = jnp.sum(window_exp, axis=1, keepdims=True) + jnp.sum(sink_exp, axis=1, keepdims=True) + self_exp
    scale = 1.0 / total
    window_prob = (window_exp * scale).astype(BF16)
    sink_prob = (sink_exp * scale).astype(BF16)
    self_prob = (self_exp * scale).astype(BF16).astype(F32)
    loads["v"].wait()
    mixture = (
        dot(window_prob, v_v[...].reshape(R * WINDOW, HD))
        + dot(sink_prob, sinks[R * SINKS :])
        + self_prob * fresh.astype(F32)
    ).astype(BF16)
    loads["outw"].wait()
    partial = dot(mixture, outw_v[...])
    for j in range(NC):
        send1[j] = partial[:, j * 256 : (j + 1) * 256].astype(BF16)
    chunk = lax.rem(m, NC)

    pl.semaphore_wait(barrier, NC + NP - 1)

    to_near_mp(lambda k: remote(0, send1.at[lax.rem(k, NC)], recv1.at[chunk], (g, d, k)))
    recv1[chunk] = send1[chunk]
    remote(8, vocab_h.at[:, pl.ds(pl.multiple_of((1 - g) * 768, HD), WIDE)], voc_v.at[own_rows, :], (1 - g, d, m))

    loads["ids"].wait()
    loads["route"].wait()
    half = m // (NZ // 2)
    own_expert = 2 * me + half
    before = (iota((HD, HD), 0) // R == iota((HD, HD), 1) // R) & (iota((HD, HD), 0) < iota((HD, HD), 1))
    before = jnp.where(before, 1.0, 0.0).astype(BF16)
    coefficients = []
    for s in range(2):
        match = ids_v[s] == own_expert
        chosen = jnp.sum(jnp.where(match, 1.0, 0.0), axis=0, keepdims=True)
        weight = jnp.sum(jnp.where(match, rw_v[s], 0.0), axis=0, keepdims=True)
        rank = dot(jnp.broadcast_to(chosen, (R, HD)).astype(BF16), before)[:1]
        rows, lanes = iota((32, HD), 0), iota((32, HD), 1)
        takes = (lanes // R == rows // 2) & (rank.astype(jnp.int32) == lax.rem(rows, 2)) & (chosen > 0.5)
        coefficients.append(jnp.sum(jnp.where(takes, weight, 0.0), axis=1, keepdims=True))
    coefficient = jnp.concatenate(coefficients, axis=0)

    own_ids = jnp.where(g == 0, ids_v[0], ids_v[1]).astype(F32).astype(BF16)
    pick = jnp.where(iota((HD, 64), 0) == d * R + lax.rem(iota((HD, 64), 1), R), 1.0, 0.0).astype(BF16)
    ids_row = dot(own_ids, pick)
    rows = iota((512, 64), 0)
    cols = iota((512, 64), 1)
    expert = (rows // 16 * 2 + half).astype(F32)
    named = jnp.zeros((512, 64), F32)
    for i in range(8):
        named = jnp.where(expert == ids_row[i : i + 1, :], 1.0, named)
    earlier = (iota((64, 64), 0) // R == iota((64, 64), 1) // R) & (iota((64, 64), 0) < iota((64, 64), 1))
    rank = dot(named.astype(BF16), jnp.where(earlier, 1.0, 0.0).astype(BF16))
    scatter = jnp.where(
        (named > 0.5) & (rank.astype(jnp.int32) == lax.rem(rows // 8, 2)) & (lax.rem(rows, 8) == cols // R), 1.0, 0.0
    ).astype(BF16)
    eye = jnp.where(iota((HD, HD), 0) == iota((HD, HD), 1), 1.0, 0.0).astype(BF16)
    ids_col = dot_nt(eye, own_ids)
    cols = iota((HD, 1024), 1)
    expert = (cols // 32 * 2 + half).astype(F32)
    named = jnp.zeros((HD, 1024), F32)
    for i in range(8):
        named = jnp.where(expert == ids_col[:, i : i + 1], 1.0, named)
    earlier = (iota((HD, HD), 0) // R == iota((HD, HD), 1) // R) & (iota((HD, HD), 1) < iota((HD, HD), 0))
    rank = dot(jnp.where(earlier, 1.0, 0.0).astype(BF16), named.astype(BF16))
    takes = (rank.astype(jnp.int32) == lax.rem(cols, 2)) & (lax.rem(cols, 32) // 2 == iota((HD, 1024), 0) // R)
    gather[...] = jnp.where(takes & (named > 0.5), 1.0, 0.0).astype(BF16)
    rows, cols = iota((64, 64), 0), iota((64, 64), 1)
    swap = jnp.where((rows // 8 == lax.rem(cols, 8)) & (lax.rem(rows, 8) == cols // 8), 1.0, 0.0).astype(BF16)

    arrived(0, recv1.at[pl.ds(0, NC - 1)])
    windows[m] = jnp.sum(recv1[...].astype(F32), axis=0).astype(BF16)

    to_mp(lambda k: remote(1, windows.at[m], windows.at[m], (g, d, k)))
    arrived(1, windows.at[pl.ds(0, NZ - 1)])
    pieces = []
    for q in range(NC):
        total = windows[q].astype(F32) + windows[q + NC].astype(F32)
        pieces.append((st_v[:, q * 256 : q * 256 + 256].astype(F32) + total).astype(BF16).astype(F32))
    squares = sum(jnp.sum(p * p, axis=1, keepdims=True) for p in pieces)
    inv = lax.rsqrt(squares / D + EPSILON)
    stacked = jnp.concatenate([p * inv for p in pieces], axis=0).astype(BF16)

    send3[...] = dot(scatter, stacked).astype(BF16).reshape(NP, 16, 256)

    to_plane(lambda p, q: remote(2, send3.at[p * ND + q], recv3.at[me], (p, q, m)))
    recv3[me] = send3[me]

    low = iota((R, HD), 1) < 64
    for j in range(NC):
        first = pieces[j // 2][:, j % 2 * HD : j % 2 * HD + HD]
        second = pieces[j // 2 + 4][:, j % 2 * HD : j % 2 * HD + HD]
        rsend[2 * j] = jnp.where(low, first, pltpu.roll(second, 64, axis=1)).astype(BF16)
        rsend[2 * j + 1] = jnp.where(low, pltpu.roll(first, 64, axis=1), second).astype(BF16)
    to_chips(lambda p, q: remote(9, rsend.at[q], rrecv.at[d], (p, q, m)))
    rrecv[d] = rsend[d]
    for name in ("ein0", "ein1", "eout"):
        loads[name].wait()
    arrived(2, recv3.at[pl.ds(0, NP - 1)])
    tokens = []
    for n in range(8):
        turned = dot(swap, recv3[4 * n : 4 * n + 4].reshape(64, 256))
        tokens.append(jnp.concatenate([turned[8 * q : 8 * q + 8] for q in range(8)], axis=1))
    tokens = jnp.concatenate(tokens, axis=0).astype(BF16)
    both = dot(tokens, ein_v[...])
    gate, upward = both[:, :HD], both[:, HD:]
    activated = (gate / (1.0 + jnp.exp(-gate)) * upward * coefficient).astype(BF16)
    terms = dot(activated, eout_v[...])
    low = iota((64, HD), 1) < 64
    for j in range(NC):
        first, second = terms[:, j * HD : j * HD + HD], terms[:, (j + NC) * HD : (j + NC) * HD + HD]
        send4[2 * j] = jnp.where(low, first, pltpu.roll(second, 64, axis=1)).astype(BF16)
        send4[2 * j + 1] = jnp.where(low, pltpu.roll(first, 64, axis=1), second).astype(BF16)

    to_plane(lambda p, q: remote(3, send4.at[q, pl.ds(pl.multiple_of(p * 32, 32), 32)], recv4.at[me], (p, q, m)))
    recv4[me] = send4[d, pl.ds(pl.multiple_of(g * 32, 32), 32)]
    arrived(3, recv4.at[pl.ds(0, NP - 1)])
    send5[...] = dot(gather[...], recv4[...].reshape(1024, HD)).astype(BF16).reshape(NC, 16, HD)

    to_mp(lambda k: remote(4, send5.at[lax.rem(k, NC)], recv5.at[m], (g, d, k)))
    recv5[m] = send5[chunk]
    arrived(9, rrecv.at[pl.ds(0, ND - 1)])
    residual = rrecv[pl.ds(2 * chunk, 2)].astype(F32).reshape(16, HD)
    arrived(4, recv5.at[pl.ds(0, NZ - 1)])
    uz[g, chunk] = (residual + jnp.sum(recv5[...].astype(F32), axis=0)).astype(BF16)

    def send_6(k):
        remote(5, uz.at[g, chunk], uz.at[g, chunk], (g, d, k))
        remote(5, uz.at[g, chunk], uz.at[g, chunk], (1 - g, d, k))

    to_near_mp(send_6)
    remote(5, uz.at[g, chunk], uz.at[g, chunk], (1 - g, d, m))
    loads["guid"].wait()
    guidance = column(gd_v[...])
    loads["vocab"].wait()
    arrived(8, voc_v.at[pl.ds(0, 64), :])
    arrived(5, recv5.at[pl.ds(0, NZ - 1)])
    sums = uz[...].reshape(2 * ND * R, HD)
    squares = jnp.sum(sums.astype(F32) * sums.astype(F32), axis=1, keepdims=True)
    upper = squares.astype(BF16).astype(F32)
    lanes = iota((2 * ND * R, HD), 1)
    marks = jnp.where(lax.rem(lanes, 64) < 32, upper, squares - upper)
    partial = dot(sums, voc_v[...])
    first = jnp.where((lanes < 64) & (g == 1), marks, partial[:, :HD])
    last = jnp.where((lanes >= 64) & (g == 0), marks, partial[:, WIDE - HD :])
    for part, start in ((first, 0), (partial[:, HD : WIDE - HD], HD), (last, WIDE - HD)):
        part = part.astype(BF16)
        for t in range(2):
            send8[:, t * R : t * R + R, start : start + part.shape[1]] = part[t * HD : t * HD + HD].reshape(
                ND, R, part.shape[1]
            )

    to_chips(lambda p, q: remote(7, send8.at[q], recv8.at[d], (p, q, m)))
    recv8[d] = send8[d]
    arrived(7, recv8.at[pl.ds(0, ND - 1)])
    logits = jnp.sum(recv8[...].astype(F32), axis=0)
    lanes = iota((2 * R, WIDE), 1)
    spare = ((lanes < 64) & (g == 1)) | ((lanes >= HALF) & (g == 0))
    squares = jnp.sum(jnp.where(spare, logits, 0.0), axis=1, keepdims=True) * (1.0 / 32)
    logits = logits * lax.rsqrt(squares / D + EPSILON)
    logits = logits[R:] + guidance * (logits[:R] - logits[R:])
    logits = jnp.where(g == 0, logits, pltpu.roll(logits, WIDE - 64, axis=1))
    for r in range(R):
        out_ref[r] = logits[r : r + 1, :HALF]

    sent(0, recv1.at[pl.ds(0, NC - 1)])
    sent(1, windows.at[pl.ds(0, NZ - 1)])
    sent(2, recv3.at[pl.ds(0, NP - 1)])
    sent(3, recv4.at[pl.ds(0, NP - 1)])
    sent(4, recv5.at[pl.ds(0, NZ - 1)])
    sent(5, recv5.at[pl.ds(0, NZ - 1)])
    sent(7, recv8.at[pl.ds(0, ND - 1)])
    sent(8, voc_v.at[pl.ds(0, 64), :])
    sent(9, rrecv.at[pl.ds(0, ND - 1)])


def body(
    states, lengths, sink_cache, window_cache, qkv_weight, out_weight, expert_ids, route_weight,
    expert_in, expert_out, vocab_weight, guidance,
):
    qkv = jnp.transpose(qkv_weight, (1, 2, 0, 3)).reshape(3, D, HD)
    ids = jnp.transpose(expert_ids, (0, 2, 1))
    route = jnp.transpose(route_weight, (0, 2, 1))
    guided = pl.pallas_call(
        kernel,
        out_shape=pltpu.VMEM((R, 1, HALF), F32),
        in_specs=[pl.BlockSpec(memory_space=pl.ANY)] * 12,
        out_specs=pl.BlockSpec(memory_space=pltpu.VMEM),
        scratch_shapes=[
            pltpu.VMEM((R, D), BF16),
            pltpu.VMEM((1, R), jnp.int32),
            pltpu.VMEM((R, 2, SINKS, HD), BF16),
            pltpu.VMEM((2 * R * SINKS, HD), F32),
            pltpu.VMEM((R, WINDOW, HD), BF16),
            pltpu.VMEM((R, WINDOW, HD), BF16),
            pltpu.VMEM((D, 3 * HD), BF16),
            pltpu.VMEM((HD, D), BF16),
            pltpu.VMEM((2, 8, HD), jnp.int32),
            pltpu.VMEM((2, 8, HD), F32),
            pltpu.VMEM((D, 2 * HD), BF16),
            pltpu.VMEM((HD, D), BF16),
            pltpu.VMEM((HD, WIDE), BF16),
            pltpu.VMEM((1, R), F32),
            pltpu.VMEM((NC, R, 256), BF16),
            pltpu.VMEM((NC, R, 256), BF16),
            pltpu.VMEM((NZ, R, 256), BF16),
            pltpu.VMEM((HD, 1024), BF16),
            pltpu.VMEM((ND, R, HD), BF16),
            pltpu.VMEM((ND, R, HD), BF16),
            pltpu.VMEM((NP, 16, 256), BF16),
            pltpu.VMEM((NP, 16, 256), BF16),
            pltpu.VMEM((ND, 64, HD), BF16),
            pltpu.VMEM((NP, 32, HD), BF16),
            pltpu.VMEM((NC, 16, HD), BF16),
            pltpu.VMEM((NZ, 16, HD), BF16),
            pltpu.VMEM((2, NC, 16, HD), BF16),
            pltpu.VMEM((ND, 16, WIDE), BF16),
            pltpu.VMEM((ND, 16, WIDE), BF16),
            pltpu.SemaphoreType.DMA((16,)),
            pltpu.SemaphoreType.DMA((10,)),
            pltpu.SemaphoreType.DMA((10,)),
        ],
        compiler_params=pltpu.CompilerParams(
            collective_id=0, has_side_effects=True, vmem_limit_bytes=56 << 20
        ),
    )(
        states, lengths, sink_cache, window_cache, qkv, out_weight, ids, route,
        expert_in, expert_out, vocab_weight, guidance.reshape(1, R),
    )
    return guided.reshape(R, 1, 1, HALF)


def solution(mesh):
    in_specs = (
        P("guide", "dp", None),
        P("guide", "dp"),
        P("guide", "dp", "mp", None, None, None),
        P("guide", "dp", "mp", None, None, None),
        P(None, None, "mp", None),
        P("mp", None, None),
        P(),
        P(),
        P(None, None, ("guide", "dp", "mp")),
        P(("guide", "dp", "mp"), None),
        P(("guide", "dp"), "mp"),
        P("dp"),
    )
    out_specs = P("dp", "mp", "guide", None)
    return jax.shard_map(body, mesh=mesh, in_specs=in_specs, out_specs=out_specs, check_vma=False)
```

```python
import math

import jax
import jax.numpy as jnp
from jax import lax
from jax.experimental import pallas as pl
from jax.experimental.pallas import tpu as pltpu
from jax.sharding import PartitionSpec as P

F32 = jnp.float32
BF16 = jnp.bfloat16
EPSILON = 1e-05
MESH = pl.DeviceIdType.MESH
D = 2048
HD = 128
R = 8
NZ = 16
ND = 16
NP = 32
NC = 8
SINKS = 4
WINDOW = 256
HALF = 832
WIDE = 896
NEG = -1e30


def iota(shape, axis):
    return lax.broadcasted_iota(jnp.int32, shape, axis)


def dot(a, b):
    return jnp.dot(a, b, preferred_element_type=F32)


def dot_nt(a, b):
    return lax.dot_general(a, b, (((1,), (1,)), ((), ())), preferred_element_type=F32)


def column(row):
    square = jnp.broadcast_to(row, (R, R))
    return jnp.sum(jnp.where(iota((R, R), 0) == iota((R, R), 1), square, 0.0), axis=1, keepdims=True)


def kernel(
    states_h, lengths_h, sink_h, window_h, qkv_h, outw_h, ids_h, route_h, ein_h, eout_h, vocab_h, guid_h,
    out_ref,
    st_v, len_v, sink_v, sinkf_v, k_v, v_v, qkv_v, outw_v, ids_v, rw_v, ein_v, eout_v, voc_v, gd_v,
    send1, recv1, windows, gather, rsend, rrecv, send3, recv3, send4, recv4, send5, recv5, uz, send8, recv8,
    local_sem, send_sem, recv_sem,
):
    g = lax.axis_index("guide")
    d = lax.axis_index("dp")
    m = lax.axis_index("mp")
    me = g * ND + d

    barrier = pltpu.get_barrier_semaphore()

    y, x = d // 4, lax.rem(d, 4)

    def turn(a):
        return jnp.where(a == 0, 2, jnp.where(a == 1, 1, jnp.where(a == 2, 3, 0)))

    def chip(i):
        return lax.rem(y + turn(i // 4), 4) * 4 + lax.rem(x + turn(lax.rem(i, 4)), 4)

    def to_chips(act):
        def step(i, carry):
            other = chip(i)
            act(g, other)
            return carry

        lax.fori_loop(0, ND - 1, step, 0)

    def to_plane(act):
        def step(i, carry):
            other = chip(i)
            act(0, other)
            act(1, other)
            return carry

        lax.fori_loop(0, ND - 1, step, 0)
        act(1 - g, d)

    def to_mp(act):
        def step(i, carry):
            offset = jnp.where(lax.rem(i, 2) == 0, 8 + i // 2, 8 - (i + 1) // 2)
            act(lax.rem(m + offset, NZ))
            return carry

        lax.fori_loop(0, NZ - 1, step, 0)

    def to_near_mp(act):
        def step(i, carry):
            offset = jnp.where(lax.rem(i, 2) == 0, 4 - i // 2, 13 + i // 2)
            act(lax.rem(m + offset, NZ))
            return carry

        lax.fori_loop(0, NC - 1, step, 0)

    def greet(device):
        pl.semaphore_signal(barrier, inc=1, device_id=device, device_id_type=MESH)

    to_near_mp(lambda k: greet((g, d, k)))
    greet((g, d, lax.rem(m + 12, NZ)))

    loads = {}

    def load(name, src, dst):
        copy = pltpu.make_async_copy(src, dst, local_sem.at[len(loads)])
        loads[name] = copy
        copy.start()

    load("states", states_h.at[0], st_v)
    load("lengths", lengths_h, len_v)
    for t in range(3):
        load("qkv%d" % t, qkv_h.at[t], qkv_v.at[:, pl.ds(t * HD, HD)])
    load("sink", sink_h.at[0, :, 0], sink_v)
    load("k", window_h.at[0, :, 0, 0], k_v)
    load("v", window_h.at[0, :, 0, 1], v_v)
    load("outw", outw_h.at[0], outw_v)
    to_plane(lambda p, q: greet((p, q, m)))
    load("ids", ids_h, ids_v)
    load("route", route_h, rw_v)
    load("ein0", ein_h.at[0], ein_v.at[:, pl.ds(0, HD)])
    load("ein1", ein_h.at[1], ein_v.at[:, pl.ds(HD, HD)])
    load("eout", eout_h, eout_v)
    own_columns = pl.ds(pl.multiple_of(g * 768, HD), WIDE)
    own_rows = pl.ds(pl.multiple_of(g * 64, 64), 64)
    load("vocab", vocab_h.at[:, own_columns], voc_v.at[own_rows, :])
    load("guid", guid_h, gd_v)

    def remote(phase, src, dst, device):
        pltpu.make_async_remote_copy(
            src_ref=src, dst_ref=dst, send_sem=send_sem.at[phase], recv_sem=recv_sem.at[phase],
            device_id=device, device_id_type=MESH,
        ).start()

    def arrived(phase, ref):
        pltpu.make_async_copy(ref, ref, recv_sem.at[phase]).wait()

    def sent(phase, ref):
        pltpu.make_async_copy(ref, ref, send_sem.at[phase]).wait()

    step_index = lax.rem(iota((1, HD), 1), HD // 2).astype(F32)
    inverse = jnp.exp(step_index * (-2.0 * math.log(10000.0) / HD))
    loads["lengths"].wait()
    position = column(len_v[...].astype(F32))
    angles = position * inverse
    cosine = jnp.cos(angles)
    sine = jnp.sin(angles)
    sine = jnp.where(iota((R, HD), 1) < HD // 2, -sine, sine)
    loads["states"].wait()
    hidden = st_v[...].astype(F32)
    normed = (hidden * lax.rsqrt(jnp.mean(hidden * hidden, axis=-1, keepdims=True) + EPSILON)).astype(BF16)
    loads["sink"].wait()
    for r in range(R):
        for t in range(2):
            sinkf_v[pl.ds(t * R * SINKS + r * SINKS, SINKS), :] = sink_v[r, t].astype(F32)
    for t in range(3):
        loads["qkv%d" % t].wait()
    projected = dot(normed, qkv_v[...])
    query = projected[:, :HD]
    key = projected[:, HD : 2 * HD]
    query = (query * cosine + pltpu.roll(query, HD // 2, axis=1) * sine).astype(BF16)
    key = (key * cosine + pltpu.roll(key, HD // 2, axis=1) * sine).astype(BF16)
    fresh = projected[:, 2 * HD :].astype(BF16)
    root = 1.0 / math.sqrt(HD)
    sinks = sinkf_v[...].astype(BF16)
    loads["k"].wait()
    window_scores = dot_nt(query, k_v[...].reshape(R * WINDOW, HD)) * root
    sink_scores = dot_nt(query, sinks[: R * SINKS]) * root
    self_scores = jnp.sum(query.astype(F32) * key.astype(F32), axis=1, keepdims=True) * root
    position_i = position.astype(jnp.int32)
    slot = iota((R, R * WINDOW), 1)
    window_ok = (slot // WINDOW == iota((R, R * WINDOW), 0)) & (
        lax.rem(slot, WINDOW) >= SINKS + WINDOW - position_i
    )
    slot = iota((R, R * SINKS), 1)
    sink_ok = (slot // SINKS == iota((R, R * SINKS), 0)) & (lax.rem(slot, SINKS) < position_i)
    window_scores = jnp.where(window_ok, window_scores, NEG)
    sink_scores = jnp.where(sink_ok, sink_scores, NEG)
    highest = jnp.maximum(
        jnp.maximum(
            jnp.max(window_scores, axis=1, keepdims=True), jnp.max(sink_scores, axis=1, keepdims=True)
        ),
        self_scores,
    )
    window_exp = jnp.where(window_ok, jnp.exp(window_scores - highest), 0.0)
    sink_exp = jnp.where(sink_ok, jnp.exp(sink_scores - highest), 0.0)
    self_exp = jnp.exp(self_scores - highest)
    total = jnp.sum(window_exp, axis=1, keepdims=True) + jnp.sum(sink_exp, axis=1, keepdims=True) + self_exp
    scale = 1.0 / total
    window_prob = (window_exp * scale).astype(BF16)
    sink_prob = (sink_exp * scale).astype(BF16)
    self_prob = (self_exp * scale).astype(BF16).astype(F32)
    loads["v"].wait()
    mixture = (
        dot(window_prob, v_v[...].reshape(R * WINDOW, HD))
        + dot(sink_prob, sinks[R * SINKS :])
        + self_prob * fresh.astype(F32)
    ).astype(BF16)
    loads["outw"].wait()
    partial = dot(mixture, outw_v[...])
    for j in range(NC):
        send1[j] = partial[:, j * 256 : (j + 1) * 256].astype(BF16)
    chunk = lax.rem(m, NC)

    pl.semaphore_wait(barrier, NC + NP - 1)

    to_near_mp(lambda k: remote(0, send1.at[lax.rem(k, NC)], recv1.at[chunk], (g, d, k)))
    recv1[chunk] = send1[chunk]
    remote(8, vocab_h.at[:, pl.ds(pl.multiple_of((1 - g) * 768, HD), WIDE)], voc_v.at[own_rows, :], (1 - g, d, m))

    loads["ids"].wait()
    loads["route"].wait()
    half = m // (NZ // 2)
    own_expert = 2 * me + half
    before = (iota((HD, HD), 0) // R == iota((HD, HD), 1) // R) & (iota((HD, HD), 0) < iota((HD, HD), 1))
    before = jnp.where(before, 1.0, 0.0).astype(BF16)
    coefficients = []
    for s in range(2):
        match = ids_v[s] == own_expert
        chosen = jnp.sum(jnp.where(match, 1.0, 0.0), axis=0, keepdims=True)
        weight = jnp.sum(jnp.where(match, rw_v[s], 0.0), axis=0, keepdims=True)
        rank = dot(jnp.broadcast_to(chosen, (R, HD)).astype(BF16), before)[:1]
        rows, lanes = iota((32, HD), 0), iota((32, HD), 1)
        takes = (lanes // R == rows // 2) & (rank.astype(jnp.int32) == lax.rem(rows, 2)) & (chosen > 0.5)
        coefficients.append(jnp.sum(jnp.where(takes, weight, 0.0), axis=1, keepdims=True))
    coefficient = jnp.concatenate(coefficients, axis=0)

    own_ids = jnp.where(g == 0, ids_v[0], ids_v[1]).astype(F32).astype(BF16)
    pick = jnp.where(iota((HD, 64), 0) == d * R + lax.rem(iota((HD, 64), 1), R), 1.0, 0.0).astype(BF16)
    ids_row = dot(own_ids, pick)
    rows = iota((512, 64), 0)
    cols = iota((512, 64), 1)
    expert = (rows // 16 * 2 + half).astype(F32)
    named = jnp.zeros((512, 64), F32)
    for i in range(8):
        named = jnp.where(expert == ids_row[i : i + 1, :], 1.0, named)
    earlier = (iota((64, 64), 0) // R == iota((64, 64), 1) // R) & (iota((64, 64), 0) < iota((64, 64), 1))
    rank = dot(named.astype(BF16), jnp.where(earlier, 1.0, 0.0).astype(BF16))
    scatter = jnp.where(
        (named > 0.5) & (rank.astype(jnp.int32) == lax.rem(rows // 8, 2)) & (lax.rem(rows, 8) == cols // R), 1.0, 0.0
    ).astype(BF16)
    rows, cols = iota((64, 64), 0), iota((64, 64), 1)
    swap = jnp.where((rows // 8 == lax.rem(cols, 8)) & (lax.rem(rows, 8) == cols // 8), 1.0, 0.0).astype(BF16)

    arrived(0, recv1.at[pl.ds(0, NC - 1)])
    windows[m] = jnp.sum(recv1[...].astype(F32), axis=0).astype(BF16)

    to_mp(lambda k: remote(1, windows.at[m], windows.at[m], (g, d, k)))

    eye = jnp.where(iota((HD, HD), 0) == iota((HD, HD), 1), 1.0, 0.0).astype(BF16)
    ids_col = dot_nt(eye, own_ids)
    cols = iota((HD, 1024), 1)
    expert = (cols // 32 * 2 + half).astype(F32)
    named = jnp.zeros((HD, 1024), F32)
    for i in range(8):
        named = jnp.where(expert == ids_col[:, i : i + 1], 1.0, named)
    earlier = (iota((HD, HD), 0) // R == iota((HD, HD), 1) // R) & (iota((HD, HD), 1) < iota((HD, HD), 0))
    rank = dot(jnp.where(earlier, 1.0, 0.0).astype(BF16), named.astype(BF16))
    takes = (rank.astype(jnp.int32) == lax.rem(cols, 2)) & (lax.rem(cols, 32) // 2 == iota((HD, 1024), 0) // R)
    gather[...] = jnp.where(takes & (named > 0.5), 1.0, 0.0).astype(BF16)
    arrived(1, windows.at[pl.ds(0, NZ - 1)])
    pieces = []
    for q in range(NC):
        total = windows[q].astype(F32) + windows[q + NC].astype(F32)
        pieces.append((st_v[:, q * 256 : q * 256 + 256].astype(F32) + total).astype(BF16).astype(F32))
    squares = sum(jnp.sum(p * p, axis=1, keepdims=True) for p in pieces)
    inv = lax.rsqrt(squares / D + EPSILON)
    stacked = jnp.concatenate([p * inv for p in pieces], axis=0).astype(BF16)

    send3[...] = dot(scatter, stacked).astype(BF16).reshape(NP, 16, 256)

    to_plane(lambda p, q: remote(2, send3.at[p * ND + q], recv3.at[me], (p, q, m)))
    recv3[me] = send3[me]

    low = iota((R, HD), 1) < 64
    for j in range(NC):
        first = pieces[j // 2][:, j % 2 * HD : j % 2 * HD + HD]
        second = pieces[j // 2 + 4][:, j % 2 * HD : j % 2 * HD + HD]
        rsend[2 * j] = jnp.where(low, first, pltpu.roll(second, 64, axis=1)).astype(BF16)
        rsend[2 * j + 1] = jnp.where(low, pltpu.roll(first, 64, axis=1), second).astype(BF16)
    for name in ("ein0", "ein1", "eout"):
        loads[name].wait()
    arrived(2, recv3.at[pl.ds(0, NP - 1)])
    tokens = []
    for n in range(8):
        turned = dot(swap, recv3[4 * n : 4 * n + 4].reshape(64, 256))
        tokens.append(jnp.concatenate([turned[8 * q : 8 * q + 8] for q in range(8)], axis=1))
    tokens = jnp.concatenate(tokens, axis=0).astype(BF16)
    both = dot(tokens, ein_v[...])
    gate, upward = both[:, :HD], both[:, HD:]
    activated = (gate / (1.0 + jnp.exp(-gate)) * upward * coefficient).astype(BF16)
    terms = dot(activated, eout_v[...])
    low = iota((64, HD), 1) < 64
    for j in range(NC):
        first, second = terms[:, j * HD : j * HD + HD], terms[:, (j + NC) * HD : (j + NC) * HD + HD]
        send4[2 * j] = jnp.where(low, first, pltpu.roll(second, 64, axis=1)).astype(BF16)
        send4[2 * j + 1] = jnp.where(low, pltpu.roll(first, 64, axis=1), second).astype(BF16)

    to_plane(lambda p, q: remote(3, send4.at[q, pl.ds(pl.multiple_of(p * 32, 32), 32)], recv4.at[me], (p, q, m)))
    recv4[me] = send4[d, pl.ds(pl.multiple_of(g * 32, 32), 32)]
    arrived(3, recv4.at[pl.ds(0, NP - 1)])
    send5[...] = dot(gather[...], recv4[...].reshape(1024, HD)).astype(BF16).reshape(NC, 16, HD)

    to_mp(lambda k: remote(4, send5.at[lax.rem(k, NC)], recv5.at[m], (g, d, k)))
    to_chips(lambda p, q: remote(9, rsend.at[q], rrecv.at[d], (p, q, m)))
    rrecv[d] = rsend[d]
    recv5[m] = send5[chunk]
    arrived(9, rrecv.at[pl.ds(0, ND - 1)])
    residual = rrecv[pl.ds(2 * chunk, 2)].astype(F32).reshape(16, HD)
    arrived(4, recv5.at[pl.ds(0, NZ - 1)])
    uz[g, chunk] = (residual + jnp.sum(recv5[...].astype(F32), axis=0)).astype(BF16)

    def send_6(k):
        remote(5, uz.at[g, chunk], uz.at[g, chunk], (g, d, k))
        remote(5, uz.at[g, chunk], uz.at[g, chunk], (1 - g, d, k))

    to_near_mp(send_6)
    remote(5, uz.at[g, chunk], uz.at[g, chunk], (1 - g, d, m))
    loads["guid"].wait()
    guidance = column(gd_v[...])
    loads["vocab"].wait()
    arrived(8, voc_v.at[pl.ds(0, 64), :])
    arrived(5, recv5.at[pl.ds(0, NZ - 1)])
    sums = uz[...].reshape(2 * ND * R, HD)
    squares = jnp.sum(sums.astype(F32) * sums.astype(F32), axis=1, keepdims=True)
    upper = squares.astype(BF16).astype(F32)
    lanes = iota((2 * ND * R, HD), 1)
    marks = jnp.where(lax.rem(lanes, 64) < 32, upper, squares - upper)
    partial = dot(sums, voc_v[...])
    first = jnp.where((lanes < 64) & (g == 1), marks, partial[:, :HD])
    last = jnp.where((lanes >= 64) & (g == 0), marks, partial[:, WIDE - HD :])
    for part, start in ((first, 0), (partial[:, HD : WIDE - HD], HD), (last, WIDE - HD)):
        part = part.astype(BF16)
        for t in range(2):
            send8[:, t * R : t * R + R, start : start + part.shape[1]] = part[t * HD : t * HD + HD].reshape(
                ND, R, part.shape[1]
            )

    to_chips(lambda p, q: remote(7, send8.at[q], recv8.at[d], (p, q, m)))
    recv8[d] = send8[d]
    arrived(7, recv8.at[pl.ds(0, ND - 1)])
    logits = jnp.sum(recv8[...].astype(F32), axis=0)
    lanes = iota((2 * R, WIDE), 1)
    spare = ((lanes < 64) & (g == 1)) | ((lanes >= HALF) & (g == 0))
    squares = jnp.sum(jnp.where(spare, logits, 0.0), axis=1, keepdims=True) * (1.0 / 32)
    logits = logits * lax.rsqrt(squares / D + EPSILON)
    logits = logits[R:] + guidance * (logits[:R] - logits[R:])
    logits = jnp.where(g == 0, logits, pltpu.roll(logits, WIDE - 64, axis=1))
    for r in range(R):
        out_ref[r] = logits[r : r + 1, :HALF]

    sent(0, recv1.at[pl.ds(0, NC - 1)])
    sent(1, windows.at[pl.ds(0, NZ - 1)])
    sent(2, recv3.at[pl.ds(0, NP - 1)])
    sent(3, recv4.at[pl.ds(0, NP - 1)])
    sent(4, recv5.at[pl.ds(0, NZ - 1)])
    sent(5, recv5.at[pl.ds(0, NZ - 1)])
    sent(7, recv8.at[pl.ds(0, ND - 1)])
    sent(8, voc_v.at[pl.ds(0, 64), :])
    sent(9, rrecv.at[pl.ds(0, ND - 1)])


def body(
    states, lengths, sink_cache, window_cache, qkv_weight, out_weight, expert_ids, route_weight,
    expert_in, expert_out, vocab_weight, guidance,
):
    qkv = jnp.transpose(qkv_weight, (1, 2, 0, 3)).reshape(3, D, HD)
    ids = jnp.transpose(expert_ids, (0, 2, 1))
    route = jnp.transpose(route_weight, (0, 2, 1))
    guided = pl.pallas_call(
        kernel,
        out_shape=pltpu.VMEM((R, 1, HALF), F32),
        in_specs=[pl.BlockSpec(memory_space=pl.ANY)] * 12,
        out_specs=pl.BlockSpec(memory_space=pltpu.VMEM),
        scratch_shapes=[
            pltpu.VMEM((R, D), BF16),
            pltpu.VMEM((1, R), jnp.int32),
            pltpu.VMEM((R, 2, SINKS, HD), BF16),
            pltpu.VMEM((2 * R * SINKS, HD), F32),
            pltpu.VMEM((R, WINDOW, HD), BF16),
            pltpu.VMEM((R, WINDOW, HD), BF16),
            pltpu.VMEM((D, 3 * HD), BF16),
            pltpu.VMEM((HD, D), BF16),
            pltpu.VMEM((2, 8, HD), jnp.int32),
            pltpu.VMEM((2, 8, HD), F32),
            pltpu.VMEM((D, 2 * HD), BF16),
            pltpu.VMEM((HD, D), BF16),
            pltpu.VMEM((HD, WIDE), BF16),
            pltpu.VMEM((1, R), F32),
            pltpu.VMEM((NC, R, 256), BF16),
            pltpu.VMEM((NC, R, 256), BF16),
            pltpu.VMEM((NZ, R, 256), BF16),
            pltpu.VMEM((HD, 1024), BF16),
            pltpu.VMEM((ND, R, HD), BF16),
            pltpu.VMEM((ND, R, HD), BF16),
            pltpu.VMEM((NP, 16, 256), BF16),
            pltpu.VMEM((NP, 16, 256), BF16),
            pltpu.VMEM((ND, 64, HD), BF16),
            pltpu.VMEM((NP, 32, HD), BF16),
            pltpu.VMEM((NC, 16, HD), BF16),
            pltpu.VMEM((NZ, 16, HD), BF16),
            pltpu.VMEM((2, NC, 16, HD), BF16),
            pltpu.VMEM((ND, 16, WIDE), BF16),
            pltpu.VMEM((ND, 16, WIDE), BF16),
            pltpu.SemaphoreType.DMA((16,)),
            pltpu.SemaphoreType.DMA((10,)),
            pltpu.SemaphoreType.DMA((10,)),
        ],
        compiler_params=pltpu.CompilerParams(
            collective_id=0, has_side_effects=True, vmem_limit_bytes=56 << 20
        ),
    )(
        states, lengths, sink_cache, window_cache, qkv, out_weight, ids, route,
        expert_in, expert_out, vocab_weight, guidance.reshape(1, R),
    )
    return guided.reshape(R, 1, 1, HALF)


def solution(mesh):
    in_specs = (
        P("guide", "dp", None),
        P("guide", "dp"),
        P("guide", "dp", "mp", None, None, None),
        P("guide", "dp", "mp", None, None, None),
        P(None, None, "mp", None),
        P("mp", None, None),
        P(),
        P(),
        P(None, None, ("guide", "dp", "mp")),
        P(("guide", "dp", "mp"), None),
        P(("guide", "dp"), "mp"),
        P("dp"),
    )
    out_specs = P("dp", "mp", "guide", None)
    return jax.shard_map(body, mesh=mesh, in_specs=in_specs, out_specs=out_specs, check_vma=False)
```

```python
import math

import jax
import jax.numpy as jnp
from jax import lax
from jax.experimental import pallas as pl
from jax.experimental.pallas import tpu as pltpu
from jax.sharding import PartitionSpec as P

F32 = jnp.float32
BF16 = jnp.bfloat16
EPSILON = 1e-05
MESH = pl.DeviceIdType.MESH
D = 2048
HD = 128
R = 8
NZ = 16
ND = 16
NP = 32
NC = 8
SINKS = 4
WINDOW = 256
HALF = 832
WIDE = 896
NEG = -1e30


def iota(shape, axis):
    return lax.broadcasted_iota(jnp.int32, shape, axis)


def dot(a, b):
    return jnp.dot(a, b, preferred_element_type=F32)


def dot_nt(a, b):
    return lax.dot_general(a, b, (((1,), (1,)), ((), ())), preferred_element_type=F32)


def column(row):
    square = jnp.broadcast_to(row, (R, R))
    return jnp.sum(jnp.where(iota((R, R), 0) == iota((R, R), 1), square, 0.0), axis=1, keepdims=True)


def kernel(
    states_h, lengths_h, sink_h, window_h, qkv_h, outw_h, ids_h, route_h, ein_h, eout_h, vocab_h, guid_h,
    out_ref,
    st_v, len_v, sink_v, sinkf_v, k_v, v_v, qkv_v, outw_v, ids_v, rw_v, ein_v, eout_v, voc_v, gd_v,
    send1, recv1, windows, gather, rsend, rrecv, send3, recv3, send4, recv4, send5, recv5, uz, send8, recv8,
    local_sem, send_sem, recv_sem,
):
    g = lax.axis_index("guide")
    d = lax.axis_index("dp")
    m = lax.axis_index("mp")
    me = g * ND + d

    barrier = pltpu.get_barrier_semaphore()

    y, x = d // 4, lax.rem(d, 4)

    def turn(a):
        return jnp.where(a == 0, 2, jnp.where(a == 1, 1, jnp.where(a == 2, 3, 0)))

    def chip(i):
        return lax.rem(y + turn(i // 4), 4) * 4 + lax.rem(x + turn(lax.rem(i, 4)), 4)

    def to_chips(act):
        def step(i, carry):
            other = chip(i)
            act(g, other)
            return carry

        lax.fori_loop(0, ND - 1, step, 0)

    def to_plane(act):
        def step(i, carry):
            other = chip(i)
            act(0, other)
            act(1, other)
            return carry

        lax.fori_loop(0, ND - 1, step, 0)
        act(1 - g, d)

    def to_mp(act):
        def step(i, carry):
            offset = jnp.where(lax.rem(i, 2) == 0, 8 + i // 2, 8 - (i + 1) // 2)
            act(lax.rem(m + offset, NZ))
            return carry

        lax.fori_loop(0, NZ - 1, step, 0)

    def to_near_mp(act):
        def step(i, carry):
            offset = jnp.where(lax.rem(i, 2) == 0, 4 - i // 2, 13 + i // 2)
            act(lax.rem(m + offset, NZ))
            return carry

        lax.fori_loop(0, NC - 1, step, 0)

    def greet(device):
        pl.semaphore_signal(barrier, inc=1, device_id=device, device_id_type=MESH)

    to_near_mp(lambda k: greet((g, d, k)))
    greet((g, d, lax.rem(m + 12, NZ)))

    loads = {}

    def load(name, src, dst):
        copy = pltpu.make_async_copy(src, dst, local_sem.at[len(loads)])
        loads[name] = copy
        copy.start()

    load("states", states_h.at[0], st_v)
    load("lengths", lengths_h, len_v)
    for t in range(3):
        load("qkv%d" % t, qkv_h.at[t], qkv_v.at[:, pl.ds(t * HD, HD)])
    load("sink", sink_h.at[0, :, 0], sink_v)
    load("k", window_h.at[0, :, 0, 0], k_v)
    load("v", window_h.at[0, :, 0, 1], v_v)
    load("outw", outw_h.at[0], outw_v)
    to_plane(lambda p, q: greet((p, q, m)))
    load("ids", ids_h, ids_v)
    load("route", route_h, rw_v)
    load("ein0", ein_h.at[0], ein_v.at[:, pl.ds(0, HD)])
    load("ein1", ein_h.at[1], ein_v.at[:, pl.ds(HD, HD)])
    load("eout", eout_h, eout_v)
    own_columns = pl.ds(pl.multiple_of(g * 768, HD), WIDE)
    own_rows = pl.ds(pl.multiple_of(g * 64, 64), 64)
    load("vocab", vocab_h.at[:, own_columns], voc_v.at[own_rows, :])
    load("guid", guid_h, gd_v)

    def remote(phase, src, dst, device):
        pltpu.make_async_remote_copy(
            src_ref=src, dst_ref=dst, send_sem=send_sem.at[phase], recv_sem=recv_sem.at[phase],
            device_id=device, device_id_type=MESH,
        ).start()

    def arrived(phase, ref):
        pltpu.make_async_copy(ref, ref, recv_sem.at[phase]).wait()

    def sent(phase, ref):
        pltpu.make_async_copy(ref, ref, send_sem.at[phase]).wait()

    step_index = lax.rem(iota((1, HD), 1), HD // 2).astype(F32)
    inverse = jnp.exp(step_index * (-2.0 * math.log(10000.0) / HD))
    loads["lengths"].wait()
    position = column(len_v[...].astype(F32))
    angles = position * inverse
    cosine = jnp.cos(angles)
    sine = jnp.sin(angles)
    sine = jnp.where(iota((R, HD), 1) < HD // 2, -sine, sine)
    loads["states"].wait()
    hidden = st_v[...].astype(F32)
    normed = (hidden * lax.rsqrt(jnp.mean(hidden * hidden, axis=-1, keepdims=True) + EPSILON)).astype(BF16)
    loads["sink"].wait()
    for r in range(R):
        for t in range(2):
            sinkf_v[pl.ds(t * R * SINKS + r * SINKS, SINKS), :] = sink_v[r, t].astype(F32)
    for t in range(3):
        loads["qkv%d" % t].wait()
    projected = dot(normed, qkv_v[...])
    query = projected[:, :HD]
    key = projected[:, HD : 2 * HD]
    query = (query * cosine + pltpu.roll(query, HD // 2, axis=1) * sine).astype(BF16)
    key = (key * cosine + pltpu.roll(key, HD // 2, axis=1) * sine).astype(BF16)
    fresh = projected[:, 2 * HD :].astype(BF16)
    root = 1.0 / math.sqrt(HD)
    sinks = sinkf_v[...].astype(BF16)
    loads["k"].wait()
    window_scores = dot_nt(query, k_v[...].reshape(R * WINDOW, HD)) * root
    sink_scores = dot_nt(query, sinks[: R * SINKS]) * root
    self_scores = jnp.sum(query.astype(F32) * key.astype(F32), axis=1, keepdims=True) * root
    position_i = position.astype(jnp.int32)
    slot = iota((R, R * WINDOW), 1)
    window_ok = (slot // WINDOW == iota((R, R * WINDOW), 0)) & (
        lax.rem(slot, WINDOW) >= SINKS + WINDOW - position_i
    )
    slot = iota((R, R * SINKS), 1)
    sink_ok = (slot // SINKS == iota((R, R * SINKS), 0)) & (lax.rem(slot, SINKS) < position_i)
    window_scores = jnp.where(window_ok, window_scores, NEG)
    sink_scores = jnp.where(sink_ok, sink_scores, NEG)
    highest = jnp.maximum(
        jnp.maximum(
            jnp.max(window_scores, axis=1, keepdims=True), jnp.max(sink_scores, axis=1, keepdims=True)
        ),
        self_scores,
    )
    window_exp = jnp.where(window_ok, jnp.exp(window_scores - highest), 0.0)
    sink_exp = jnp.where(sink_ok, jnp.exp(sink_scores - highest), 0.0)
    self_exp = jnp.exp(self_scores - highest)
    total = jnp.sum(window_exp, axis=1, keepdims=True) + jnp.sum(sink_exp, axis=1, keepdims=True) + self_exp
    scale = 1.0 / total
    window_prob = (window_exp * scale).astype(BF16)
    sink_prob = (sink_exp * scale).astype(BF16)
    self_prob = (self_exp * scale).astype(BF16).astype(F32)
    loads["v"].wait()
    mixture = (
        dot(window_prob, v_v[...].reshape(R * WINDOW, HD))
        + dot(sink_prob, sinks[R * SINKS :])
        + self_prob * fresh.astype(F32)
    ).astype(BF16)
    loads["outw"].wait()
    partial = dot(mixture, outw_v[...])
    for j in range(NC):
        send1[j] = partial[:, j * 256 : (j + 1) * 256].astype(BF16)
    chunk = lax.rem(m, NC)

    pl.semaphore_wait(barrier, NC + NP - 1)

    to_near_mp(lambda k: remote(0, send1.at[lax.rem(k, NC)], recv1.at[chunk], (g, d, k)))
    recv1[chunk] = send1[chunk]
    remote(8, vocab_h.at[:, pl.ds(pl.multiple_of((1 - g) * 768, HD), WIDE)], voc_v.at[own_rows, :], (1 - g, d, m))

    loads["ids"].wait()
    loads["route"].wait()
    half = m // (NZ // 2)
    own_expert = 2 * me + half
    before = (iota((HD, HD), 0) // R == iota((HD, HD), 1) // R) & (iota((HD, HD), 0) < iota((HD, HD), 1))
    before = jnp.where(before, 1.0, 0.0).astype(BF16)
    coefficients = []
    for s in range(2):
        match = ids_v[s] == own_expert
        chosen = jnp.sum(jnp.where(match, 1.0, 0.0), axis=0, keepdims=True)
        weight = jnp.sum(jnp.where(match, rw_v[s], 0.0), axis=0, keepdims=True)
        rank = dot(jnp.broadcast_to(chosen, (R, HD)).astype(BF16), before)[:1]
        rows, lanes = iota((32, HD), 0), iota((32, HD), 1)
        takes = (lanes // R == rows // 2) & (rank.astype(jnp.int32) == lax.rem(rows, 2)) & (chosen > 0.5)
        coefficients.append(jnp.sum(jnp.where(takes, weight, 0.0), axis=1, keepdims=True))
    coefficient = jnp.concatenate(coefficients, axis=0)

    own_ids = jnp.where(g == 0, ids_v[0], ids_v[1]).astype(F32).astype(BF16)
    pick = jnp.where(iota((HD, 64), 0) == d * R + lax.rem(iota((HD, 64), 1), R), 1.0, 0.0).astype(BF16)
    ids_row = dot(own_ids, pick)
    rows = iota((512, 64), 0)
    cols = iota((512, 64), 1)
    expert = (rows // 16 * 2 + half).astype(F32)
    named = jnp.zeros((512, 64), F32)
    for i in range(8):
        named = jnp.where(expert == ids_row[i : i + 1, :], 1.0, named)
    earlier = (iota((64, 64), 0) // R == iota((64, 64), 1) // R) & (iota((64, 64), 0) < iota((64, 64), 1))
    rank = dot(named.astype(BF16), jnp.where(earlier, 1.0, 0.0).astype(BF16))
    scatter = jnp.where(
        (named > 0.5) & (rank.astype(jnp.int32) == lax.rem(rows // 8, 2)) & (lax.rem(rows, 8) == cols // R), 1.0, 0.0
    ).astype(BF16)
    eye = jnp.where(iota((HD, HD), 0) == iota((HD, HD), 1), 1.0, 0.0).astype(BF16)
    ids_col = dot_nt(eye, own_ids)
    cols = iota((HD, 1024), 1)
    expert = (cols // 32 * 2 + half).astype(F32)
    named = jnp.zeros((HD, 1024), F32)
    for i in range(8):
        named = jnp.where(expert == ids_col[:, i : i + 1], 1.0, named)
    earlier = (iota((HD, HD), 0) // R == iota((HD, HD), 1) // R) & (iota((HD, HD), 1) < iota((HD, HD), 0))
    rank = dot(jnp.where(earlier, 1.0, 0.0).astype(BF16), named.astype(BF16))
    takes = (rank.astype(jnp.int32) == lax.rem(cols, 2)) & (lax.rem(cols, 32) // 2 == iota((HD, 1024), 0) // R)
    gather[...] = jnp.where(takes & (named > 0.5), 1.0, 0.0).astype(BF16)
    rows, cols = iota((64, 64), 0), iota((64, 64), 1)
    swap = jnp.where((rows // 8 == lax.rem(cols, 8)) & (lax.rem(rows, 8) == cols // 8), 1.0, 0.0).astype(BF16)

    arrived(0, recv1.at[pl.ds(0, NC - 1)])
    windows[m] = jnp.sum(recv1[...].astype(F32), axis=0).astype(BF16)

    to_mp(lambda k: remote(1, windows.at[m], windows.at[m], (g, d, k)))
    arrived(1, windows.at[pl.ds(0, NZ - 1)])
    pieces = []
    for q in range(NC):
        total = windows[q].astype(F32) + windows[q + NC].astype(F32)
        pieces.append((st_v[:, q * 256 : q * 256 + 256].astype(F32) + total).astype(BF16).astype(F32))
    squares = sum(jnp.sum(p * p, axis=1, keepdims=True) for p in pieces)
    inv = lax.rsqrt(squares / D + EPSILON)
    stacked = jnp.concatenate([p * inv for p in pieces], axis=0).astype(BF16)

    send3[...] = dot(scatter, stacked).astype(BF16).reshape(NP, 16, 256)

    to_plane(lambda p, q: remote(2, send3.at[p * ND + q], recv3.at[me], (p, q, m)))
    recv3[me] = send3[me]

    low = iota((R, HD), 1) < 64
    for j in range(NC):
        first = pieces[j // 2][:, j % 2 * HD : j % 2 * HD + HD]
        second = pieces[j // 2 + 4][:, j % 2 * HD : j % 2 * HD + HD]
        rsend[2 * j] = jnp.where(low, first, pltpu.roll(second, 64, axis=1)).astype(BF16)
        rsend[2 * j + 1] = jnp.where(low, pltpu.roll(first, 64, axis=1), second).astype(BF16)
    for name in ("ein0", "ein1", "eout"):
        loads[name].wait()
    arrived(2, recv3.at[pl.ds(0, NP - 1)])
    tokens = []
    for n in range(8):
        turned = dot(swap, recv3[4 * n : 4 * n + 4].reshape(64, 256))
        tokens.append(jnp.concatenate([turned[8 * q : 8 * q + 8] for q in range(8)], axis=1))
    tokens = jnp.concatenate(tokens, axis=0).astype(BF16)
    both = dot(tokens, ein_v[...])
    gate, upward = both[:, :HD], both[:, HD:]
    activated = (gate / (1.0 + jnp.exp(-gate)) * upward * coefficient).astype(BF16)
    terms = dot(activated, eout_v[...])
    low = iota((64, HD), 1) < 64
    for j in range(NC):
        first, second = terms[:, j * HD : j * HD + HD], terms[:, (j + NC) * HD : (j + NC) * HD + HD]
        send4[2 * j] = jnp.where(low, first, pltpu.roll(second, 64, axis=1)).astype(BF16)
        send4[2 * j + 1] = jnp.where(low, pltpu.roll(first, 64, axis=1), second).astype(BF16)

    to_plane(lambda p, q: remote(3, send4.at[q, pl.ds(pl.multiple_of(p * 32, 32), 32)], recv4.at[me], (p, q, m)))
    recv4[me] = send4[d, pl.ds(pl.multiple_of(g * 32, 32), 32)]
    arrived(3, recv4.at[pl.ds(0, NP - 1)])
    send5[...] = dot(gather[...], recv4[...].reshape(1024, HD)).astype(BF16).reshape(NC, 16, HD)

    to_mp(lambda k: remote(4, send5.at[lax.rem(k, NC)], recv5.at[m], (g, d, k)))
    to_chips(lambda p, q: remote(9, rsend.at[q], rrecv.at[d], (p, q, m)))
    rrecv[d] = rsend[d]
    recv5[m] = send5[chunk]
    arrived(9, rrecv.at[pl.ds(0, ND - 1)])
    residual = rrecv[pl.ds(2 * chunk, 2)].astype(F32).reshape(16, HD)
    arrived(4, recv5.at[pl.ds(0, NZ - 1)])
    uz[g, chunk] = (residual + jnp.sum(recv5[...].astype(F32), axis=0)).astype(BF16)

    def send_6(k):
        remote(5, uz.at[g, chunk], uz.at[g, chunk], (g, d, k))
        remote(5, uz.at[g, chunk], uz.at[g, chunk], (1 - g, d, k))

    to_near_mp(send_6)
    remote(5, uz.at[g, chunk], uz.at[g, chunk], (1 - g, d, m))
    loads["guid"].wait()
    guidance = column(gd_v[...])
    loads["vocab"].wait()
    arrived(8, voc_v.at[pl.ds(0, 64), :])
    arrived(5, recv5.at[pl.ds(0, NZ - 1)])
    lanes = iota((ND * R, HD), 1)
    for t in range(2):
        sums = uz[t].reshape(ND * R, HD)
        squares = jnp.sum(sums.astype(F32) * sums.astype(F32), axis=1, keepdims=True)
        upper = squares.astype(BF16).astype(F32)
        marks = jnp.where(lax.rem(lanes, 64) < 32, upper, squares - upper)
        partial = dot(sums, voc_v[...])
        first = jnp.where((lanes < 64) & (g == 1), marks, partial[:, :HD])
        last = jnp.where((lanes >= 64) & (g == 0), marks, partial[:, WIDE - HD :])
        for part, start in ((first, 0), (partial[:, HD : WIDE - HD], HD), (last, WIDE - HD)):
            width = part.shape[1]
            send8[t, :, :, start : start + width] = part.astype(BF16).reshape(ND, R, width)

        to_chips(lambda p, q: remote(6 + t, send8.at[t, q], recv8.at[t, d], (p, q, m)))
    for t in range(2):
        recv8[t, d] = send8[t, d]
    lanes = iota((R, WIDE), 1)
    spare = ((lanes < 64) & (g == 1)) | ((lanes >= HALF) & (g == 0))
    streams = []
    for t in range(2):
        arrived(6 + t, recv8.at[t, pl.ds(0, ND - 1)])
        logits = jnp.sum(recv8[t].astype(F32), axis=0)
        squares = jnp.sum(jnp.where(spare, logits, 0.0), axis=1, keepdims=True) * (1.0 / 32)
        streams.append(logits * lax.rsqrt(squares / D + EPSILON))
    logits = streams[1] + guidance * (streams[0] - streams[1])
    logits = jnp.where(g == 0, logits, pltpu.roll(logits, WIDE - 64, axis=1))
    for r in range(R):
        out_ref[r] = logits[r : r + 1, :HALF]

    sent(0, recv1.at[pl.ds(0, NC - 1)])
    sent(1, windows.at[pl.ds(0, NZ - 1)])
    sent(2, recv3.at[pl.ds(0, NP - 1)])
    sent(3, recv4.at[pl.ds(0, NP - 1)])
    sent(4, recv5.at[pl.ds(0, NZ - 1)])
    sent(5, recv5.at[pl.ds(0, NZ - 1)])
    for t in range(2):
        sent(6 + t, recv8.at[t, pl.ds(0, ND - 1)])
    sent(8, voc_v.at[pl.ds(0, 64), :])
    sent(9, rrecv.at[pl.ds(0, ND - 1)])


def body(
    states, lengths, sink_cache, window_cache, qkv_weight, out_weight, expert_ids, route_weight,
    expert_in, expert_out, vocab_weight, guidance,
):
    qkv = jnp.transpose(qkv_weight, (1, 2, 0, 3)).reshape(3, D, HD)
    ids = jnp.transpose(expert_ids, (0, 2, 1))
    route = jnp.transpose(route_weight, (0, 2, 1))
    guided = pl.pallas_call(
        kernel,
        out_shape=pltpu.VMEM((R, 1, HALF), F32),
        in_specs=[pl.BlockSpec(memory_space=pl.ANY)] * 12,
        out_specs=pl.BlockSpec(memory_space=pltpu.VMEM),
        scratch_shapes=[
            pltpu.VMEM((R, D), BF16),
            pltpu.VMEM((1, R), jnp.int32),
            pltpu.VMEM((R, 2, SINKS, HD), BF16),
            pltpu.VMEM((2 * R * SINKS, HD), F32),
            pltpu.VMEM((R, WINDOW, HD), BF16),
            pltpu.VMEM((R, WINDOW, HD), BF16),
            pltpu.VMEM((D, 3 * HD), BF16),
            pltpu.VMEM((HD, D), BF16),
            pltpu.VMEM((2, 8, HD), jnp.int32),
            pltpu.VMEM((2, 8, HD), F32),
            pltpu.VMEM((D, 2 * HD), BF16),
            pltpu.VMEM((HD, D), BF16),
            pltpu.VMEM((HD, WIDE), BF16),
            pltpu.VMEM((1, R), F32),
            pltpu.VMEM((NC, R, 256), BF16),
            pltpu.VMEM((NC, R, 256), BF16),
            pltpu.VMEM((NZ, R, 256), BF16),
            pltpu.VMEM((HD, 1024), BF16),
            pltpu.VMEM((ND, R, HD), BF16),
            pltpu.VMEM((ND, R, HD), BF16),
            pltpu.VMEM((NP, 16, 256), BF16),
            pltpu.VMEM((NP, 16, 256), BF16),
            pltpu.VMEM((ND, 64, HD), BF16),
            pltpu.VMEM((NP, 32, HD), BF16),
            pltpu.VMEM((NC, 16, HD), BF16),
            pltpu.VMEM((NZ, 16, HD), BF16),
            pltpu.VMEM((2, NC, 16, HD), BF16),
            pltpu.VMEM((2, ND, R, WIDE), BF16),
            pltpu.VMEM((2, ND, R, WIDE), BF16),
            pltpu.SemaphoreType.DMA((16,)),
            pltpu.SemaphoreType.DMA((10,)),
            pltpu.SemaphoreType.DMA((10,)),
        ],
        compiler_params=pltpu.CompilerParams(
            collective_id=0, has_side_effects=True, vmem_limit_bytes=56 << 20
        ),
    )(
        states, lengths, sink_cache, window_cache, qkv, out_weight, ids, route,
        expert_in, expert_out, vocab_weight, guidance.reshape(1, R),
    )
    return guided.reshape(R, 1, 1, HALF)


def solution(mesh):
    in_specs = (
        P("guide", "dp", None),
        P("guide", "dp"),
        P("guide", "dp", "mp", None, None, None),
        P("guide", "dp", "mp", None, None, None),
        P(None, None, "mp", None),
        P("mp", None, None),
        P(),
        P(),
        P(None, None, ("guide", "dp", "mp")),
        P(("guide", "dp", "mp"), None),
        P(("guide", "dp"), "mp"),
        P("dp"),
    )
    out_specs = P("dp", "mp", "guide", None)
    return jax.shard_map(body, mesh=mesh, in_specs=in_specs, out_specs=out_specs, check_vma=False)
```
